32 devices in a mesh: cells: 8 (over z, y), feat: 4 (over x, core).
Axes of the slice: x: 2, y: 2, z: 4, core: 2. Of those that a mesh axis runs over, the one named last changes fastest.
Arguments:
- expression: bfloat16 [256, 16384], P('feat', 'cells'), may hold values from -6 to 6
- tiles: bfloat16 [128, 8, 128, 128], P('cells'), may hold values from 0.0009994507 to 1
- tile_cols: int32 [128, 8], P('cells'), may hold values from 0 to 127, as said below
- tile_counts: int32 [128], P('cells'), may hold values from 3 to 8
- archetypes: int32 [48], replicated, may hold values from 0 to 16383, as said below
Outputs:
- diffused: bfloat16 [256, 16384], P('feat', 'cells')
- coords: float32 [48, 16384], P(None, 'cells')
The draws below stay inside these ranges and needn't reach their ends.
Inputs may be any that keep to these rules, and one draw needn't show every extreme that they name: tile_cols[b, 0] = b; slots 1 and 2 hold b - 16 and b + 16 in either order, one that is not a block replaced by the other; every entry lies within 16 of b; slots j >= tile_counts[b] hold b. `archetypes`: distinct cells.
All inputs are finite; a program needn't handle non-finite values.
Results may differ from the reference program's by a relative error of at most 0.0159.
Values may be sent and summed in bfloat16 or wider, within the bound.
No kernel may reach another device: no remote copies, remote signals or barrier semaphores. Data moves between devices by JAX's collectives and lax.ppermute only.
A program may use at most 64 MiB of HBM per device.

```python
import math
import jax
import jax.numpy as jnp
from jax import lax

F = 256
TILE = 128
NBT = 8
NARCH = 48
BPD = 16
BLOCKS = 128
NC = 16384


def counts_common(key):
    block_ids = jnp.arange(BLOCKS, dtype=jnp.int32)
    level = jax.random.randint(jax.random.fold_in(key, 7), (BLOCKS,), 0, NBT - 2)
    spread_sq = max((NBT - 3) * (NBT - 3), 1)
    counts = 3 + level * level * level // spread_sq
    counts = jnp.minimum(counts, NBT)
    counts = jnp.where(block_ids % 5 == 0, NBT, jnp.where(block_ids % 5 == 1, 3, counts))
    return counts.astype(jnp.int32)


def draw_tile_counts(key, part):
    return counts_common(key)


def draw_tile_cols(key, part):
    block_ids = jnp.arange(BLOCKS, dtype=jnp.int32)
    offsets = jax.random.randint(jax.random.fold_in(key, 9), (BLOCKS, NBT), -BPD, BPD + 1)
    columns = jnp.clip(block_ids[:, None] + offsets, 0, BLOCKS - 1)
    lower_block = jnp.where(block_ids - BPD >= 0, block_ids - BPD, block_ids + BPD)
    upper_block = jnp.where(block_ids + BPD <= BLOCKS - 1, block_ids + BPD, block_ids - BPD)
    flipped = jax.random.randint(jax.random.fold_in(key, 13), (BLOCKS,), 0, 2)
    slot_one = jnp.where(flipped == 1, upper_block, lower_block)
    slot_two = jnp.where(flipped == 1, lower_block, upper_block)
    columns = columns.at[:, 0].set(block_ids).at[:, 1].set(slot_one).at[:, 2].set(slot_two)
    counts = counts_common(key)
    slots = jnp.arange(NBT, dtype=jnp.int32)[None, :]
    columns = jnp.where(slots < counts[:, None], columns, block_ids[:, None])
    return columns.astype(jnp.int32)


def draw_archetypes(key, part):
    order = jax.random.permutation(jax.random.fold_in(key, 11), NC)
    return order[:NARCH].astype(jnp.int32)


def steps_of(key, shape, cuts, smallest, largest):
    factor_of, own = 1.0, jax.random.fold_in(key, 6)
    for axis_at, shards_of in cuts:
        heights = jnp.exp(jax.random.uniform(jax.random.fold_in(own, axis_at), (shards_of,), jnp.float32, smallest / len(cuts), largest / len(cuts)))
        factor_of = factor_of * jnp.repeat(heights, shape[axis_at] // shards_of).reshape([-1 if axis == axis_at else 1 for axis in range(len(shape))])
    return factor_of


def noise(rng, shape, spread, reach, shards=(), kind=jnp.bfloat16):
    values = jax.random.normal(rng, shape, jnp.float32) * spread
    if len(shards) > 0:
        values = steps_of(rng, shape, shards, -0.22, 0.18) * values
    return jnp.clip(values, min=-reach, max=reach).astype(kind)


def setup_inputs(seed: int = 0) -> dict:
    key_list = jax.random.split(jax.random.key(seed), 6)
    return {
        "expression": noise(key_list[0], (F, NC), 1.0, 6.0, ((0, 4), (1, 8))),
        "tiles": jnp.clip(jnp.exp(math.log(1.0) - 6.9083047 * jax.random.uniform(key_list[1], (BLOCKS, NBT, TILE, TILE), jnp.float32) ** steps_of(key_list[1], (BLOCKS, NBT, TILE, TILE), ((0, 8),), -0.2, 0.2)), 0.0009994507, 1.0).astype(jnp.bfloat16),
        "tile_cols": draw_tile_cols(jax.random.fold_in(key_list[5], 71), 0),
        "tile_counts": draw_tile_counts(jax.random.fold_in(key_list[5], 71), 0),
        "archetypes": draw_archetypes(jax.random.fold_in(key_list[5], 71), 0),
    }


def diffuse(matrix, tiles, tile_cols, keep):
    grid = matrix.reshape(F, BLOCKS, TILE)

    def one_block(args):
        tile, columns, kept = args
        picked = jnp.take(grid, columns, axis=1).astype(jnp.float32) * kept[None, :, None]
        weights = tile.astype(jnp.float32)
        degree = jnp.einsum('jrc,j->r', weights, kept)
        return jnp.einsum('fjc,jrc->fr', picked, weights) / degree[None, :]
    result = lax.map(one_block, (tiles, tile_cols, keep))
    return jnp.transpose(result, (1, 0, 2)).reshape(F, NC).astype(jnp.bfloat16)

def reference(expression, tiles, tile_cols, tile_counts, archetypes):
    keep = (jnp.arange(NBT, dtype=jnp.int32)[None, :] < tile_counts[:, None]).astype(jnp.float32)
    first = diffuse(expression, tiles, tile_cols, keep)
    diffused = diffuse(first, tiles, tile_cols, keep)
    arch = jnp.take(diffused, archetypes, axis=1).T
    gram = jnp.dot(arch.astype(jnp.float32), arch.T.astype(jnp.float32), preferred_element_type=jnp.float32)
    lower = jnp.linalg.cholesky(gram)
    proj = jnp.dot(arch.astype(jnp.float32), diffused.astype(jnp.float32), preferred_element_type=jnp.float32)
    values = diffused.astype(jnp.float32)
    squares = lax.optimization_barrier(jnp.sum(values * values, axis=0))
    solved = lax.linalg.triangular_solve(lower, proj, left_side=True, lower=True)
    coords = solved * lax.rsqrt(squares / F + 1e-05)[None, :]
    return (diffused, coords)
```

```python
import functools
import jax
import jax.numpy as jnp
from jax import lax
from jax.experimental import pallas as pl
from jax.experimental.pallas import tpu as pltpu
from jax.sharding import PartitionSpec as P

F = 256
TILE = 128
NBT = 8
EPS = 1e-05

VMEM = pl.BlockSpec(memory_space=pltpu.VMEM)
SMEM = pl.BlockSpec(memory_space=pltpu.SMEM)
LAST = (((1,), (1,)), ((), ()))


def dot_last(a, b):
    return lax.dot_general(a, b, LAST, preferred_element_type=jnp.float32)


def lanes(block):
    return pl.ds(pl.multiple_of(block * TILE, TILE), TILE)


def wide_tile(tiles_ref, b, slots):
    return jnp.concatenate([tiles_ref[b, j] for j in slots], axis=1)


def own_kernel(with_degree, meta_ref, cols_ref, counts_ref, tiles_ref, v_ref, acc_ref, *deg_ref):
    blocks = tiles_ref.shape[0]
    first_block = meta_ref[0]
    feats = v_ref.shape[0]
    for b in range(blocks):
        parts = []
        slots = [j for j in range(NBT) if j not in (1, 2)] if not with_degree else list(range(NBT))
        ones = []
        for j in slots:
            local = cols_ref[b, j] - first_block
            used = j < counts_ref[b]
            mine = jnp.logical_and(used, jnp.logical_and(local >= 0, local < blocks))
            x = v_ref[:, lanes(jnp.clip(local, 0, blocks - 1))]
            parts.append(jnp.where(mine, x, jnp.zeros_like(x)))
            ones.append(jnp.full((16, TILE), jnp.where(used, 1.0, 0.0), jnp.float32).astype(jnp.bfloat16))
        wide = wide_tile(tiles_ref, b, slots)
        lhs = jnp.concatenate(parts, axis=1)
        if with_degree:
            lhs = jnp.concatenate([lhs, jnp.concatenate(ones, axis=1)], axis=0)
        out = dot_last(lhs, wide)
        acc_ref[:, b * TILE:(b + 1) * TILE] = out[:feats]
        if with_degree:
            deg_ref[0][b] = out[feats:feats + 8]


def rest_kernel(meta_ref, cols_ref, counts_ref, tiles_ref, even_ref, odd_ref, acc_ref, deg_ref, out_ref):
    blocks = tiles_ref.shape[0]
    first_block, odd = meta_ref[0], meta_ref[1]
    feats = acc_ref.shape[0]
    for b in range(blocks):
        parts = []
        slots = list(range(1, NBT))
        for j in slots:
            local = cols_ref[b, j] - first_block
            lower, upper = local < 0, local >= blocks
            used = jnp.logical_and(j < counts_ref[b], jnp.logical_or(lower, upper))
            at = jnp.where(lower, local + blocks, jnp.where(upper, local - blocks, 0))
            partner = jnp.where(odd == 1, lower, upper)
            x = jnp.where(partner, even_ref[:, lanes(at)], odd_ref[:, lanes(at)])
            parts.append(jnp.where(used, x, jnp.zeros_like(x)))
        out = dot_last(jnp.concatenate(parts, axis=1), wide_tile(tiles_ref, b, slots))
        out = out + acc_ref[:, b * TILE:(b + 1) * TILE]
        out = out / deg_ref[b][:1]
        out_ref[:, b * TILE:(b + 1) * TILE] = out.astype(jnp.bfloat16)


def call(kernel, out_shape, n_smem, args, flops, nbytes):
    single = not isinstance(out_shape, (list, tuple))
    return pl.pallas_call(
        kernel,
        out_shape=out_shape,
        in_specs=[SMEM] * n_smem + [VMEM] * (len(args) - n_smem),
        out_specs=VMEM if single else [VMEM] * len(out_shape),
        compiler_params=pltpu.CompilerParams(vmem_limit_bytes=32 << 20),
        cost_estimate=pl.CostEstimate(flops=flops, bytes_accessed=nbytes, transcendentals=0),
    )(*args)


def exchange(matrix):
    size = lax.axis_size("cells")
    pairs = [(i, i ^ 1) for i in range(size)]
    others = [(i, i + 1) for i in range(1, size - 1, 2)]
    others = others + [(j, i) for i, j in others]
    return lax.ppermute(matrix, "cells", pairs), lax.ppermute(matrix, "cells", others)


def solve_kernel(a0, a1, a2, a3, q_ref, work_ref):
    pieces = [a0, a1, a2, a3]
    n = a0.shape[0]
    gram = sum(dot_last(p[...], p[...]) for p in pieces)
    row = lax.broadcasted_iota(jnp.int32, (n, n), 0)
    col = lax.broadcasted_iota(jnp.int32, (n, n), 1)
    aug = jnp.concatenate([gram, jnp.where(row == col, 1.0, 0.0)], axis=1)
    rows = lax.broadcasted_iota(jnp.int32, (n, 1), 0)
    for k in range(n):
        pivot = aug[k:k + 1, :]
        inv = lax.rsqrt(pivot[:, k:k + 1])
        inv = inv * (1.5 - 0.5 * pivot[:, k:k + 1] * inv * inv)
        scaled = pivot * inv
        factor = aug[:, k:k + 1] * inv
        aug = jnp.where(rows == k, scaled, jnp.where(rows > k, aug - factor * scaled, aug))
    inverse = aug[:, n:]
    high = inverse.astype(jnp.bfloat16)
    low = (inverse - high.astype(jnp.float32)).astype(jnp.bfloat16)
    lower = (inverse - high.astype(jnp.float32) - low.astype(jnp.float32)).astype(jnp.bfloat16)
    lhs = jnp.concatenate([high, low, lower], axis=0)
    for i, p in enumerate(pieces):
        q = lax.dot_general(lhs, p[...], (((1,), (0,)), ((), ())), preferred_element_type=jnp.float32)
        q = q[:n] + q[n:2 * n] + q[2 * n:]
        q_high = q.astype(jnp.bfloat16)
        q_low = (q - q_high.astype(jnp.float32)).astype(jnp.bfloat16)
        q_ref[i] = jnp.concatenate([q_high, q_low], axis=0)


def finish_kernel(meta_ref, q_ref, d0, d1, d2, d3, out_ref):
    n = out_ref.shape[0]
    width = out_ref.shape[1]
    me = meta_ref[2]
    flip1, flip2 = (me & 1) == 1, (me & 2) == 2
    q = jnp.concatenate([q_ref[i] for i in range(4)], axis=1)
    step = 256
    for c in range(0, width, step):
        p = [d[:, c:c + step] for d in (d0, d1, d2, d3)]
        p = [jnp.where(flip1, p[i ^ 1], p[i]) for i in range(4)]
        p = [jnp.where(flip2, p[i ^ 2], p[i]) for i in range(4)]
        d = jnp.concatenate(p, axis=0)
        z = lax.dot_general(q, d, (((1,), (0,)), ((), ())), preferred_element_type=jnp.float32)
        wide = d.astype(jnp.float32)
        sq = jnp.sum(wide * wide, axis=0, keepdims=True)
        out_ref[:, c:c + step] = (z[:n] + z[n:]) * lax.rsqrt(sq / F + EPS)


def gather_feat(x):
    size = lax.axis_size("feat")
    near = lax.ppermute(x, "feat", [(i, i ^ 1) for i in range(size)])
    far = lax.ppermute(x, "feat", [(i, i ^ 2) for i in range(size)])
    both = lax.ppermute(far, "feat", [(i, i ^ 1) for i in range(size)])
    return x, near, far, both


def on_device(expression, tiles, tile_cols, tile_counts, archetypes):
    blocks = tiles.shape[0]
    feats, rows = expression.shape
    narch = archetypes.shape[0]
    cell, feat = lax.axis_index("cells"), lax.axis_index("feat")
    meta = jnp.stack([cell * blocks, cell & 1, feat]).astype(jnp.int32)
    tile_flops = 2 * feats * TILE * TILE * NBT * blocks
    tile_bytes = 2 * TILE * TILE * NBT * blocks
    scalars = (meta, tile_cols, tile_counts)
    acc_shape = jax.ShapeDtypeStruct((feats, rows), jnp.float32)

    pair, other = exchange(expression)
    acc, degree = call(
        functools.partial(own_kernel, True),
        [acc_shape, jax.ShapeDtypeStruct((blocks, 8, TILE), jnp.float32)],
        3, (*scalars, tiles, expression), tile_flops, tile_bytes)
    out_bf16 = jax.ShapeDtypeStruct((feats, rows), jnp.bfloat16)
    first = call(rest_kernel, out_bf16, 3, (*scalars, tiles, pair, other, acc, degree), tile_flops, tile_bytes)
    pair, other = exchange(first)
    acc = call(functools.partial(own_kernel, False), acc_shape, 3, (*scalars, tiles, first), tile_flops, tile_bytes)
    diffused = call(rest_kernel, out_bf16, 3, (*scalars, tiles, pair, other, acc, degree), tile_flops, tile_bytes)

    pieces = gather_feat(diffused)

    local_ids = archetypes - cell * rows
    selector = (local_ids[:, None] == jnp.arange(rows, dtype=jnp.int32)[None, :]).astype(jnp.bfloat16)
    picked = lax.dot_general(selector, diffused, LAST, preferred_element_type=jnp.float32)
    picked = picked.astype(jnp.bfloat16)
    size = lax.axis_size("cells")
    spread = lax.all_to_all(jnp.broadcast_to(picked[None], (size, *picked.shape)), "cells", 0, 0)
    arch = jnp.sum(spread.astype(jnp.float32), axis=0).astype(jnp.bfloat16)
    near = lax.ppermute(arch, "feat", [(i, i ^ 1) for i in range(4)])
    far = lax.ppermute(arch, "feat", [(i, i ^ 2) for i in range(4)])
    both = lax.ppermute(arch, "feat", [(i, i ^ 3) for i in range(4)])
    parts = [arch, near, far, both]
    parts = [jnp.where((feat & 1) == 1, parts[i ^ 1], parts[i]) for i in range(4)]
    parts = [jnp.where((feat & 2) == 2, parts[i ^ 2], parts[i]) for i in range(4)]
    q = pl.pallas_call(
        solve_kernel,
        out_shape=jax.ShapeDtypeStruct((4, 2 * narch, feats), jnp.bfloat16),
        in_specs=[VMEM] * 4, out_specs=VMEM,
        scratch_shapes=[pltpu.VMEM((narch, 2 * narch), jnp.float32)],
        cost_estimate=pl.CostEstimate(flops=1 << 20, bytes_accessed=1 << 17, transcendentals=0),
    )(*parts)
    coords = call(finish_kernel, jax.ShapeDtypeStruct((narch, rows), jnp.float32), 1,
                  (meta, q, *pieces), 2 * 2 * narch * F * rows, 4 * narch * rows)
    return diffused, coords


def solution(mesh):
    return jax.shard_map(
        on_device,
        mesh=mesh,
        in_specs=(
            P("feat", "cells"),
            P("cells", None, None, None),
            P("cells", None),
            P("cells"),
            P(),
        ),
        out_specs=(P("feat", "cells"), P(None, "cells")),
        check_vma=False,
    )
```

```python
import functools
import jax
import jax.numpy as jnp
from jax import lax
from jax.experimental import pallas as pl
from jax.experimental.pallas import tpu as pltpu
from jax.sharding import PartitionSpec as P

F = 256
TILE = 128
NBT = 8
EPS = 1e-05
COLS, ARCH, COUNTS, META = range(4)

VMEM = pl.BlockSpec(memory_space=pltpu.VMEM)
SMEM = pl.BlockSpec(memory_space=pltpu.SMEM)
ANY = pl.BlockSpec(memory_space=pl.ANY)
HBM = pl.BlockSpec(memory_space=pltpu.HBM)


def dot_last(a, b):
    return lax.dot_general(a, b, (((1,), (1,)), ((), ())), preferred_element_type=jnp.float32)


def dot(a, b):
    return lax.dot_general(a, b, (((1,), (0,)), ((), ())), preferred_element_type=jnp.float32)


def lanes(block):
    return pl.ds(pl.multiple_of(block * TILE, TILE), TILE)


def wide_tile(tiles_ref, b, slots):
    return jnp.concatenate([tiles_ref[b, j] for j in slots], axis=1)


def halves(x):
    high = x.astype(jnp.bfloat16)
    return high, (x - high.astype(jnp.float32)).astype(jnp.bfloat16)


def column(row, narch):
    at = lax.broadcasted_iota(jnp.int32, (narch, narch), 0) == lax.broadcasted_iota(jnp.int32, (narch, narch), 1)
    return jnp.sum(jnp.where(at, row.astype(jnp.float32), 0.0), axis=1, keepdims=True).astype(jnp.int32)


def rows_kernel(info_ref, table_ref, tiles_ref, rows_ref, held_ref, sem):
    blocks = tiles_ref.shape[0]
    narch = rows_ref.shape[0]
    first_block, first_slot = info_ref[META, 0], 2 * info_ref[META, 2]
    copies = []
    for i in range(2):
        copies.append(pltpu.make_async_copy(tiles_ref.at[:, first_slot + i], held_ref.at[:, i], sem.at[i]))
        copies[-1].start()
    local = column(table_ref[ARCH:ARCH + 1, :narch], narch) - first_block * TILE
    at = lax.broadcasted_iota(jnp.int32, (narch, TILE), 1)
    hits = [(local - b * TILE) == at for b in range(blocks)]
    owner = lax.broadcasted_iota(jnp.int32, (narch, blocks), 1) == lax.div(local, TILE)
    owner = jnp.where(jnp.logical_and(owner, local >= 0), 1.0, 0.0).astype(jnp.bfloat16)
    cols = jnp.concatenate([table_ref[COLS:COLS + 1, j * blocks:(j + 1) * blocks] for j in range(NBT)], axis=0)
    steps = cols - first_block - lax.broadcasted_iota(jnp.int32, cols.shape, 1)
    steps = dot_last(owner, steps.astype(jnp.float32).astype(jnp.bfloat16))
    rows_ref[:, 2 * TILE:] = jnp.zeros((narch, TILE), jnp.bfloat16)
    rows_ref[:, 2 * TILE:2 * TILE + NBT] = steps.astype(jnp.bfloat16)
    for i in range(2):
        sel = [
            jnp.where(hit, jnp.where(first_slot + i < info_ref[COUNTS, b], 1.0, 0.0), 0.0).astype(jnp.bfloat16)
            for b, hit in enumerate(hits)
        ]
        copies[i].wait()
        tall = jnp.concatenate([held_ref[b, i] for b in range(blocks)], axis=0)
        row = dot(jnp.concatenate(sel, axis=1), tall)
        rows_ref[:, i * TILE:(i + 1) * TILE] = row.astype(jnp.bfloat16)


def step_block(info_ref, tiles_ref, own_ref, pair_ref, other_ref, b, with_degree):
    blocks = own_ref.shape[1] // TILE
    first_block, odd = info_ref[META, 0], info_ref[META, 1]
    parts, ones = [], []
    for j in range(NBT):
        local = info_ref[COLS, j * blocks + b] - first_block
        lower, upper = local < 0, local >= blocks
        at = lanes(jnp.where(lower, local + blocks, jnp.where(upper, local - blocks, local)))
        used = j < info_ref[COUNTS, b]
        x = own_ref[:, at]
        if j > 0:
            near = jnp.logical_or(jnp.logical_and(lower, odd == 1), jnp.logical_and(upper, odd == 0))
            beside = jnp.where(near, pair_ref[:, at], other_ref[:, at])
            x = beside if j < 3 else jnp.where(jnp.logical_or(lower, upper), beside, x)
        if j >= 3:
            x = jnp.where(used, x, jnp.zeros_like(x))
        parts.append(x)
        ones.append(jnp.full((16, TILE), jnp.where(used, 1.0, 0.0), jnp.float32).astype(jnp.bfloat16))
    lhs = jnp.concatenate(parts, axis=1)
    if with_degree:
        lhs = jnp.concatenate([lhs, jnp.concatenate(ones, axis=1)], axis=0)
    return dot_last(lhs, jnp.concatenate([tiles_ref[b, j] for j in range(NBT)], axis=1))


def first_kernel(info_ref, tiles_ref, own_ref, pair_ref, other_ref, out_ref, inv_ref):
    feats = own_ref.shape[0]
    for b in range(tiles_ref.shape[0]):
        out = step_block(info_ref, tiles_ref, own_ref, pair_ref, other_ref, b, True)
        inv = 1.0 / out[feats:feats + 8]
        inv_ref[b] = inv
        out_ref[:, b * TILE:(b + 1) * TILE] = (out[:feats] * inv[:1]).astype(jnp.bfloat16)


def second_kernel(begin, info_ref, tiles_ref, own_ref, pair_ref, other_ref, inv_ref, extra_ref, out_ref):
    for i in range(out_ref.shape[1] // TILE):
        b = begin + i
        out = step_block(info_ref, tiles_ref, own_ref, pair_ref, other_ref, b, False)
        out_ref[:, i * TILE:(i + 1) * TILE] = (out * inv_ref[b][:1]).astype(jnp.bfloat16)


def arch_kernel(info_ref, table_ref, r0, r1, r2, r3, v_ref, out_ref):
    blocks = v_ref.shape[1] // TILE
    narch = r0.shape[0]
    me = info_ref[META, 2]
    block = lax.div(column(table_ref[ARCH:ARCH + 1, :narch], narch), TILE) - info_ref[META, 0]
    offsets = r0[:, 2 * TILE:].astype(jnp.float32)
    lane = lax.broadcasted_iota(jnp.int32, offsets.shape, 1)
    rows, places = [], []
    for p, r in enumerate((r0, r1, r2, r3)):
        for i in range(2):
            rows.append(r[:, i * TILE:(i + 1) * TILE].astype(jnp.float32))
            here = jnp.where(lane == 2 * (me ^ p) + i, offsets, 0.0)
            places.append(jnp.sum(here, axis=1, keepdims=True).astype(jnp.int32) + block)
    degree = jnp.sum(sum(rows), axis=1, keepdims=True)
    inv = jnp.where(degree > 0.0, 1.0 / degree, 0.0)
    rows = [r * inv for r in rows]
    weights = []
    for b in range(blocks):
        w = jnp.zeros((narch, TILE), jnp.float32)
        for r, place in zip(rows, places):
            w = w + jnp.where(place == b, r, 0.0)
        weights.append(jnp.concatenate(halves(w), axis=0))
    both = dot_last(jnp.concatenate(weights, axis=1), v_ref[...])
    part = both[:narch] + both[narch:]
    half = narch // 2
    out_ref[...] = jnp.concatenate([part[:half], part[half:]], axis=1)


def splat(x, shape):
    return jnp.broadcast_to(x, shape)


def solve_kernel(info_ref, a_ref, b_ref, d0, d1, q_ref, copy_ref):
    total = (a_ref[...] + b_ref[...]).astype(jnp.bfloat16)
    feats, half = d0.shape
    n = total.shape[0] // 2
    copy_ref[:, :half] = d0[...]
    copy_ref[:, half:] = d1[...]
    part = n // 2
    pieces = [total[p * part:(p + 1) * part] for p in range(4)]
    pieces = [jnp.concatenate([p[:, :feats], p[:, feats:]], axis=0) for p in pieces]
    pieces = in_order(info_ref[META, 2], pieces)
    arch = jnp.concatenate(pieces, axis=1)
    shape = (n, TILE)
    row = lax.broadcasted_iota(jnp.int32, shape, 0)
    col = lax.broadcasted_iota(jnp.int32, shape, 1)
    aug = jnp.concatenate([dot_last(arch, arch), jnp.zeros((n, TILE - n), jnp.float32)], axis=1)
    aug = aug + jnp.where(row + n == col, 1.0, 0.0)
    scale = jnp.zeros(shape, jnp.float32)
    group = 4
    for start in range(0, n, group):
        columns = [splat(aug[:, start + m:start + m + 1], shape) for m in range(group)]
        for m in range(group):
            k = start + m
            pivot = splat(columns[m][k:k + 1], shape)
            scale = jnp.where(row == k, pivot, scale)
            factor = jnp.where(row > k, columns[m] * (1.0 / pivot), 0.0)
            for later in range(m + 1, group):
                columns[later] = columns[later] - factor * splat(columns[later][k:k + 1], shape)
            aug = aug - factor * splat(aug[k:k + 1], shape)
    inverse = aug[:, n:2 * n] / jnp.sqrt(scale[:, :n])
    high, low = halves(inverse)
    third = (inverse - high.astype(jnp.float32) - low.astype(jnp.float32)).astype(jnp.bfloat16)
    q = dot(jnp.concatenate([high, low, third], axis=0), arch)
    high, low = halves(q[:n] + q[n:2 * n] + q[2 * n:])
    q_ref[:n] = high
    q_ref[n:] = low


def in_order(me, pieces):
    for bit in (1, 2):
        flip = (me & bit) == bit
        pieces = [jnp.where(flip, pieces[i ^ bit], pieces[i]) for i in range(4)]
    return pieces


def finish_kernel(info_ref, q_ref, *refs):
    pieces, out_ref = refs[:-1], refs[-1]
    n = out_ref.shape[0]
    half = pieces[0].shape[1]
    me = info_ref[META, 2]
    step = 256
    for h in range(2):
        for c in range(0, half, step):
            d = jnp.concatenate(in_order(me, [d[:, c:c + step] for d in pieces[4 * h:4 * h + 4]]), axis=0)
            z = dot(q_ref[...], d)
            wide = d.astype(jnp.float32)
            sq = jnp.sum(wide * wide, axis=0, keepdims=True)
            at = h * half + c
            out_ref[:, at:at + step] = (z[:n] + z[n:]) * lax.rsqrt(sq / F + EPS)


def call(kernel, out_shape, kinds, args, flops, nbytes, scratch=(), limit=16):
    single = not isinstance(out_shape, (list, tuple))
    spec = {"s": SMEM, "v": VMEM, "a": ANY, "h": HBM}
    return pl.pallas_call(
        kernel,
        out_shape=out_shape,
        in_specs=[spec[k] for k in kinds],
        out_specs=VMEM if single else [VMEM] * len(out_shape),
        scratch_shapes=scratch,
        compiler_params=pltpu.CompilerParams(vmem_limit_bytes=limit << 20),
        cost_estimate=pl.CostEstimate(flops=flops, bytes_accessed=nbytes, transcendentals=0),
    )(*args)


def exchange(matrix):
    size = lax.axis_size("cells")
    pairs = [(i, i ^ 1) for i in range(size)]
    others = [(i, i + 1) for i in range(1, size - 1, 2)]
    others = others + [(j, i) for i, j in others]
    return lax.ppermute(matrix, "cells", pairs), lax.ppermute(matrix, "cells", others)


def flip_feat(x, bits):
    return lax.ppermute(x, "feat", [(i, i ^ bits) for i in range(lax.axis_size("feat"))])


def on_device(expression, tiles, tile_cols, tile_counts, archetypes):
    blocks = tiles.shape[0]
    feats, rows = expression.shape
    narch = archetypes.shape[0]
    size = lax.axis_size("cells")
    cell, feat = lax.axis_index("cells"), lax.axis_index("feat")
    shape = jax.ShapeDtypeStruct
    bf16, f32 = jnp.bfloat16, jnp.float32
    line = lambda x: jnp.pad(x.reshape(-1), (0, TILE - x.size))
    numbers = jnp.stack([cell * blocks, cell & 1, feat]).astype(jnp.int32)
    info = jnp.concatenate([line(tile_cols.T), line(archetypes), line(tile_counts), line(numbers)]).reshape(4, TILE)
    flops = 2 * feats * TILE * TILE * NBT * blocks
    nbytes = 2 * TILE * TILE * NBT * blocks
    half = rows // 2
    half_shape = shape((feats, half), bf16)

    pair, other = exchange(expression)
    arch_rows = call(rows_kernel, shape((narch, 3 * TILE), bf16), "svh", (info, info, tiles), 0, 0,
                     [pltpu.VMEM((blocks, 2, TILE, TILE), bf16), pltpu.SemaphoreType.DMA((2,))], 52)
    first, inv = call(first_kernel, [shape((feats, rows), bf16), shape((blocks, 8, TILE), f32)], "svvvv",
                      (info, tiles, expression, pair, other), flops, nbytes)

    row_pair, row_other = exchange(arch_rows)
    own_rows, _ = lax.optimization_barrier((arch_rows, pair))
    near_rows, _ = lax.optimization_barrier((own_rows + row_pair + row_other, first))
    r = [near_rows] + [flip_feat(near_rows, p) for p in (1, 2, 3)]
    pair, other = exchange(first)
    part = call(arch_kernel, shape((narch // 2, 2 * feats), f32), "svvvvvv", (info, info, *r, first), 0, 0)
    part = jnp.concatenate([part] + [flip_feat(part, p) for p in (1, 2, 3)], axis=0)
    step = (info, tiles, first, pair, other, inv, part)
    left = call(functools.partial(second_kernel, 0), half_shape, "svvvvva", step, flops * 16, 0)
    right = call(functools.partial(second_kernel, blocks // 2), half_shape, "svvvvva", step, flops // 2, nbytes // 2)

    pieces = []
    for d in (left, right):
        near, far = flip_feat(d, 1), flip_feat(d, 2)
        pieces += [d, near, far, flip_feat(far, 1)]
    sums = (part, jnp.zeros_like(part))
    for level in range((size - 1).bit_length()):
        total = sums[0] + sums[1] if level else part
        sums = (total, lax.ppermute(total, "cells", [(i, i ^ (1 << level)) for i in range(size)]))
    q, diffused = call(solve_kernel, [shape((2 * narch, 4 * feats), bf16), shape((feats, rows), bf16)], "svvvv",
                       (info, *sums, left, right), 1 << 24, 1 << 19)
    coords = call(finish_kernel, shape((narch, rows), f32), "sv" + "v" * 8, (info, q, *pieces),
                  4 * narch * F * rows, 4 * narch * rows)
    return diffused, coords


def solution(mesh):
    return jax.shard_map(
        on_device,
        mesh=mesh,
        in_specs=(
            P("feat", "cells"),
            P("cells", None, None, None),
            P("cells", None),
            P("cells"),
            P(),
        ),
        out_specs=(P("feat", "cells"), P(None, "cells")),
        check_vma=False,
    )
```

```python
import functools
import jax
import jax.numpy as jnp
from jax import lax
from jax.experimental import pallas as pl
from jax.experimental.pallas import tpu as pltpu
from jax.sharding import PartitionSpec as P

F = 256
TILE = 128
NBT = 8
EPS = 1e-05
COLS, ARCH, COUNTS, META = range(4)

VMEM = pl.BlockSpec(memory_space=pltpu.VMEM)
SMEM = pl.BlockSpec(memory_space=pltpu.SMEM)
ANY = pl.BlockSpec(memory_space=pl.ANY)
HBM = pl.BlockSpec(memory_space=pltpu.HBM)


def dot_last(a, b):
    return lax.dot_general(a, b, (((1,), (1,)), ((), ())), preferred_element_type=jnp.float32)


def dot(a, b):
    return lax.dot_general(a, b, (((1,), (0,)), ((), ())), preferred_element_type=jnp.float32)


def lanes(block):
    return pl.ds(pl.multiple_of(block * TILE, TILE), TILE)


def wide_tile(tiles_ref, b, slots):
    return jnp.concatenate([tiles_ref[b, j] for j in slots], axis=1)


def halves(x):
    high = x.astype(jnp.bfloat16)
    return high, (x - high.astype(jnp.float32)).astype(jnp.bfloat16)


def column(row, narch):
    at = lax.broadcasted_iota(jnp.int32, (narch, narch), 0) == lax.broadcasted_iota(jnp.int32, (narch, narch), 1)
    return jnp.sum(jnp.where(at, row.astype(jnp.float32), 0.0), axis=1, keepdims=True).astype(jnp.int32)


def rows_kernel(info_ref, table_ref, tiles_ref, v_ref, rows_ref, own_ref, held_ref, sem):
    blocks = tiles_ref.shape[0]
    narch = rows_ref.shape[0]
    first_block, first_slot = info_ref[META, 0], 2 * info_ref[META, 2]
    whole = pltpu.make_async_copy(v_ref, own_ref, sem.at[2])
    whole.start()
    copies = []
    for i in range(2):
        copies.append(pltpu.make_async_copy(tiles_ref.at[:, first_slot + i], held_ref.at[:, i], sem.at[i]))
        copies[-1].start()
    local = column(table_ref[ARCH:ARCH + 1, :narch], narch) - first_block * TILE
    at = lax.broadcasted_iota(jnp.int32, (narch, TILE), 1)
    hits = [(local - b * TILE) == at for b in range(blocks)]
    owner = lax.broadcasted_iota(jnp.int32, (narch, blocks), 1) == lax.div(local, TILE)
    owner = jnp.where(jnp.logical_and(owner, local >= 0), 1.0, 0.0).astype(jnp.bfloat16)
    cols = jnp.concatenate([table_ref[COLS:COLS + 1, j * blocks:(j + 1) * blocks] for j in range(NBT)], axis=0)
    steps = cols - first_block - lax.broadcasted_iota(jnp.int32, cols.shape, 1)
    steps = dot_last(owner, steps.astype(jnp.float32).astype(jnp.bfloat16))
    rows_ref[:, 2 * TILE:] = jnp.zeros((narch, TILE), jnp.bfloat16)
    rows_ref[:, 2 * TILE:2 * TILE + NBT] = steps.astype(jnp.bfloat16)
    for i in range(2):
        sel = [
            jnp.where(hit, jnp.where(first_slot + i < info_ref[COUNTS, b], 1.0, 0.0), 0.0).astype(jnp.bfloat16)
            for b, hit in enumerate(hits)
        ]
        copies[i].wait()
        tall = jnp.concatenate([held_ref[b, i] for b in range(blocks)], axis=0)
        row = dot(jnp.concatenate(sel, axis=1), tall)
        rows_ref[:, i * TILE:(i + 1) * TILE] = row.astype(jnp.bfloat16)
    whole.wait()


def step_block(info_ref, tiles_ref, own_ref, pair_ref, other_ref, b, with_degree):
    blocks = own_ref.shape[1] // TILE
    first_block, odd = info_ref[META, 0], info_ref[META, 1]
    parts, ones = [], []
    for j in range(NBT):
        local = info_ref[COLS, j * blocks + b] - first_block
        lower, upper = local < 0, local >= blocks
        at = lanes(jnp.where(lower, local + blocks, jnp.where(upper, local - blocks, local)))
        used = j < info_ref[COUNTS, b]
        x = own_ref[:, at]
        if j > 0:
            near = jnp.logical_or(jnp.logical_and(lower, odd == 1), jnp.logical_and(upper, odd == 0))
            beside = jnp.where(near, pair_ref[:, at], other_ref[:, at])
            x = beside if j < 3 else jnp.where(jnp.logical_or(lower, upper), beside, x)
        if j >= 3:
            x = jnp.where(used, x, jnp.zeros_like(x))
        parts.append(x)
        ones.append(jnp.full((16, TILE), jnp.where(used, 1.0, 0.0), jnp.float32).astype(jnp.bfloat16))
    lhs = jnp.concatenate(parts, axis=1)
    if with_degree:
        lhs = jnp.concatenate([lhs, jnp.concatenate(ones, axis=1)], axis=0)
    return dot_last(lhs, jnp.concatenate([tiles_ref[b, j] for j in range(NBT)], axis=1))


def first_kernel(info_ref, tiles_ref, own_ref, pair_ref, other_ref, out_ref, inv_ref):
    feats = own_ref.shape[0]
    for b in range(tiles_ref.shape[0]):
        out = step_block(info_ref, tiles_ref, own_ref, pair_ref, other_ref, b, True)
        inv = 1.0 / out[feats:feats + 8]
        inv_ref[b] = inv
        out_ref[:, b * TILE:(b + 1) * TILE] = (out[:feats] * inv[:1]).astype(jnp.bfloat16)


def second_kernel(begin, info_ref, tiles_ref, own_ref, pair_ref, other_ref, inv_ref, extra_ref, out_ref):
    for i in range(out_ref.shape[1] // TILE):
        b = begin + i
        out = step_block(info_ref, tiles_ref, own_ref, pair_ref, other_ref, b, False)
        out_ref[:, i * TILE:(i + 1) * TILE] = (out * inv_ref[b][:1]).astype(jnp.bfloat16)


def arch_kernel(info_ref, table_ref, r0, r1, r2, r3, v_ref, out_ref):
    blocks = v_ref.shape[1] // TILE
    narch = r0.shape[0]
    me = info_ref[META, 2]
    block = lax.div(column(table_ref[ARCH:ARCH + 1, :narch], narch), TILE) - info_ref[META, 0]
    offsets = r0[:, 2 * TILE:].astype(jnp.float32)
    lane = lax.broadcasted_iota(jnp.int32, offsets.shape, 1)
    rows, places = [], []
    for p, r in enumerate((r0, r1, r2, r3)):
        for i in range(2):
            rows.append(r[:, i * TILE:(i + 1) * TILE].astype(jnp.float32))
            here = jnp.where(lane == 2 * (me ^ p) + i, offsets, 0.0)
            places.append(jnp.sum(here, axis=1, keepdims=True).astype(jnp.int32) + block)
    degree = jnp.sum(sum(rows), axis=1, keepdims=True)
    inv = jnp.where(degree > 0.0, 1.0 / degree, 0.0)
    rows = [r * inv for r in rows]
    weights = []
    for b in range(blocks):
        w = jnp.zeros((narch, TILE), jnp.float32)
        for r, place in zip(rows, places):
            w = w + jnp.where(place == b, r, 0.0)
        weights.append(jnp.concatenate(halves(w), axis=0))
    both = dot_last(jnp.concatenate(weights, axis=1), v_ref[...])
    part = both[:narch] + both[narch:]
    half = narch // 2
    out_ref[...] = jnp.concatenate([part[:half], part[half:]], axis=1)


def splat(x, shape):
    return jnp.broadcast_to(x, shape)


def solve_kernel(info_ref, total_ref, d0, d1, q_ref, copy_ref):
    total = total_ref[...].astype(jnp.bfloat16)
    feats, half = d0.shape
    n = total.shape[0] // 2
    copy_ref[:, :half] = d0[...]
    copy_ref[:, half:] = d1[...]
    part = n // 2
    pieces = [total[p * part:(p + 1) * part] for p in range(4)]
    pieces = [jnp.concatenate([p[:, :feats], p[:, feats:]], axis=0) for p in pieces]
    pieces = in_order(info_ref[META, 2], pieces)
    arch = jnp.concatenate(pieces, axis=1)
    shape = (n, TILE)
    row = lax.broadcasted_iota(jnp.int32, shape, 0)
    col = lax.broadcasted_iota(jnp.int32, shape, 1)
    aug = jnp.concatenate([dot_last(arch, arch), jnp.zeros((n, TILE - n), jnp.float32)], axis=1)
    aug = aug + jnp.where(row + n == col, 1.0, 0.0)
    scale = jnp.zeros(shape, jnp.float32)
    group = 4
    for start in range(0, n, group):
        columns = [splat(aug[:, start + m:start + m + 1], shape) for m in range(group)]
        for m in range(group):
            k = start + m
            pivot = splat(columns[m][k:k + 1], shape)
            scale = jnp.where(row == k, pivot, scale)
            factor = jnp.where(row > k, columns[m] * (1.0 / pivot), 0.0)
            for later in range(m + 1, group):
                columns[later] = columns[later] - factor * splat(columns[later][k:k + 1], shape)
            aug = aug - factor * splat(aug[k:k + 1], shape)
    inverse = aug[:, n:2 * n] / jnp.sqrt(scale[:, :n])
    high, low = halves(inverse)
    third = (inverse - high.astype(jnp.float32) - low.astype(jnp.float32)).astype(jnp.bfloat16)
    q = dot(jnp.concatenate([high, low, third], axis=0), arch)
    high, low = halves(q[:n] + q[n:2 * n] + q[2 * n:])
    q_ref[:n] = high
    q_ref[n:] = low


def in_order(me, pieces):
    for bit in (1, 2):
        flip = (me & bit) == bit
        pieces = [jnp.where(flip, pieces[i ^ bit], pieces[i]) for i in range(4)]
    return pieces


def finish_kernel(info_ref, q_ref, *refs):
    pieces, out_ref = refs[:-1], refs[-1]
    n = out_ref.shape[0]
    half = pieces[0].shape[1]
    me = info_ref[META, 2]
    step = 256
    for h in range(2):
        for c in range(0, half, step):
            d = jnp.concatenate(in_order(me, [d[:, c:c + step] for d in pieces[4 * h:4 * h + 4]]), axis=0)
            z = dot(q_ref[...], d)
            wide = d.astype(jnp.float32)
            sq = jnp.sum(wide * wide, axis=0, keepdims=True)
            at = h * half + c
            out_ref[:, at:at + step] = (z[:n] + z[n:]) * lax.rsqrt(sq / F + EPS)


def call(kernel, out_shape, kinds, args, flops, nbytes, scratch=(), limit=16):
    single = not isinstance(out_shape, (list, tuple))
    spec = {"s": SMEM, "v": VMEM, "a": ANY, "h": HBM}
    return pl.pallas_call(
        kernel,
        out_shape=out_shape,
        in_specs=[spec[k] for k in kinds],
        out_specs=VMEM if single else [VMEM] * len(out_shape),
        scratch_shapes=scratch,
        compiler_params=pltpu.CompilerParams(vmem_limit_bytes=limit << 20),
        cost_estimate=pl.CostEstimate(flops=flops, bytes_accessed=nbytes, transcendentals=0),
    )(*args)


def exchange(matrix):
    size = lax.axis_size("cells")
    pairs = [(i, i ^ 1) for i in range(size)]
    others = [(i, i + 1) for i in range(1, size - 1, 2)]
    others = others + [(j, i) for i, j in others]
    return lax.ppermute(matrix, "cells", pairs), lax.ppermute(matrix, "cells", others)


def flip_feat(x, bits):
    return lax.ppermute(x, "feat", [(i, i ^ bits) for i in range(lax.axis_size("feat"))])


def on_device(expression, tiles, tile_cols, tile_counts, archetypes):
    blocks = tiles.shape[0]
    feats, rows = expression.shape
    narch = archetypes.shape[0]
    size = lax.axis_size("cells")
    cell, feat = lax.axis_index("cells"), lax.axis_index("feat")
    shape = jax.ShapeDtypeStruct
    bf16, f32 = jnp.bfloat16, jnp.float32
    line = lambda x: jnp.pad(x.reshape(-1), (0, TILE - x.size))
    numbers = jnp.stack([cell * blocks, cell & 1, feat]).astype(jnp.int32)
    info = jnp.concatenate([line(tile_cols.T), line(archetypes), line(tile_counts), line(numbers)]).reshape(4, TILE)
    flops = 2 * feats * TILE * TILE * NBT * blocks
    nbytes = 2 * TILE * TILE * NBT * blocks
    half = rows // 2
    half_shape = shape((feats, half), bf16)

    pair, other = exchange(expression)
    arch_rows, own = call(rows_kernel, [shape((narch, 3 * TILE), bf16), shape((feats, rows), bf16)], "svhh",
                     (info, info, tiles, expression), 0, 0,
                     [pltpu.VMEM((blocks, 2, TILE, TILE), bf16), pltpu.SemaphoreType.DMA((3,))], 52)
    first, inv = call(first_kernel, [shape((feats, rows), bf16), shape((blocks, 8, TILE), f32)], "svvvv",
                      (info, tiles, own, pair, other), flops, nbytes)

    row_pair, row_other = exchange(arch_rows)
    own_rows, _ = lax.optimization_barrier((arch_rows, pair))
    near_rows, _ = lax.optimization_barrier((own_rows + row_pair + row_other, first))
    r = [near_rows] + [flip_feat(near_rows[:, :2 * TILE], p) for p in (1, 2, 3)]
    pair, other = exchange(first)
    part = call(arch_kernel, shape((narch // 2, 2 * feats), f32), "svvvvvv", (info, info, *r, first), 0, 0)
    partial = part
    part = jnp.concatenate([part] + [flip_feat(part, p) for p in (1, 2, 3)], axis=0)
    levels = (size - 1).bit_length()
    flip_cells = lambda x, bits: lax.ppermute(x, "cells", [(i, i ^ bits) for i in range(size)])
    level = levels % 2
    summed = part
    seen = flip_cells(part, 1) if level else None
    step = (info, tiles, first, pair, other, inv)
    left = call(functools.partial(second_kernel, 0), half_shape, "svvvvva", (*step, summed), flops * 16, 0)
    if level:
        seen, left = lax.optimization_barrier((seen, left))
        part = part + seen
    right = call(functools.partial(second_kernel, blocks // 2), half_shape, "svvvvva", (*step, part),
                 flops // 2, nbytes // 2)

    pieces = []
    for d in (left, right):
        near, far = flip_feat(d, 1), flip_feat(d, 2)
        pieces += [d, near, far, flip_feat(far, 1)]
    while level < levels:
        near, far, both = (flip_cells(part, b << level) for b in (1, 2, 3))
        part = (part + near) + (far + both)
        level += 2
    q, diffused = call(solve_kernel, [shape((2 * narch, 4 * feats), bf16), shape((feats, rows), bf16)], "svvv",
                       (info, part, left, right), 1 << 24, 1 << 19)
    coords = call(finish_kernel, shape((narch, rows), f32), "sv" + "v" * 8, (info, q, *pieces),
                  4 * narch * F * rows, 4 * narch * rows)
    return diffused, coords


def solution(mesh):
    return jax.shard_map(
        on_device,
        mesh=mesh,
        in_specs=(
            P("feat", "cells"),
            P("cells", None, None, None),
            P("cells", None),
            P("cells"),
            P(),
        ),
        out_specs=(P("feat", "cells"), P(None, "cells")),
        check_vma=False,
    )
```

```python
import functools
import jax
import jax.numpy as jnp
from jax import lax
from jax.experimental import pallas as pl
from jax.experimental.pallas import tpu as pltpu
from jax.sharding import PartitionSpec as P

F = 256
TILE = 128
NBT = 8
EPS = 1e-05
ARCH, COUNTS, META = range(NBT, NBT + 3)

VMEM = pl.BlockSpec(memory_space=pltpu.VMEM)
SMEM = pl.BlockSpec(memory_space=pltpu.SMEM)
ANY = pl.BlockSpec(memory_space=pl.ANY)
HBM = pl.BlockSpec(memory_space=pltpu.HBM)


def dot_last(a, b):
    return lax.dot_general(a, b, (((1,), (1,)), ((), ())), preferred_element_type=jnp.float32)


def dot(a, b):
    return lax.dot_general(a, b, (((1,), (0,)), ((), ())), preferred_element_type=jnp.float32)


def lanes(block):
    return pl.ds(pl.multiple_of(block * TILE, TILE), TILE)


def wide_tile(tiles_ref, b, slots):
    return jnp.concatenate([tiles_ref[b, j] for j in slots], axis=1)


def halves(x):
    high = x.astype(jnp.bfloat16)
    return high, (x - high.astype(jnp.float32)).astype(jnp.bfloat16)


def column(row, narch):
    at = lax.broadcasted_iota(jnp.int32, (narch, narch), 0) == lax.broadcasted_iota(jnp.int32, (narch, narch), 1)
    return jnp.sum(jnp.where(at, row.astype(jnp.float32), 0.0), axis=1, keepdims=True).astype(jnp.int32)


def rows_kernel(info_ref, table_ref, tiles_ref, v_ref, rows_ref, own_ref, held_ref, sem):
    blocks = tiles_ref.shape[0]
    narch = rows_ref.shape[0]
    first_block, first_slot = info_ref[META, 0], 2 * info_ref[META, 2]
    whole = pltpu.make_async_copy(v_ref, own_ref, sem.at[2])
    whole.start()
    copies = []
    for i in range(2):
        copies.append(pltpu.make_async_copy(tiles_ref.at[:, first_slot + i], held_ref.at[:, i], sem.at[i]))
        copies[-1].start()
    local = column(table_ref[ARCH:ARCH + 1, :narch], narch) - first_block * TILE
    at = lax.broadcasted_iota(jnp.int32, (narch, TILE), 1)
    hits = [(local - b * TILE) == at for b in range(blocks)]
    owner = lax.broadcasted_iota(jnp.int32, (narch, blocks), 1) == lax.div(local, TILE)
    owner = jnp.where(jnp.logical_and(owner, local >= 0), 1.0, 0.0).astype(jnp.bfloat16)
    cols = table_ref[:NBT, :blocks]
    steps = cols - first_block - lax.broadcasted_iota(jnp.int32, cols.shape, 1)
    steps = dot_last(owner, steps.astype(jnp.float32).astype(jnp.bfloat16))
    rows_ref[:, 2 * TILE:] = jnp.zeros((narch, TILE), jnp.bfloat16)
    rows_ref[:, 2 * TILE:2 * TILE + NBT] = steps.astype(jnp.bfloat16)
    for i in range(2):
        sel = [
            jnp.where(hit, jnp.where(first_slot + i < info_ref[COUNTS, b], 1.0, 0.0), 0.0).astype(jnp.bfloat16)
            for b, hit in enumerate(hits)
        ]
        copies[i].wait()
        tall = jnp.concatenate([held_ref[b, i] for b in range(blocks)], axis=0)
        row = dot(jnp.concatenate(sel, axis=1), tall)
        rows_ref[:, i * TILE:(i + 1) * TILE] = row.astype(jnp.bfloat16)
    whole.wait()


def step_block(info_ref, tiles_ref, own_ref, pair_ref, other_ref, b, with_degree):
    blocks = own_ref.shape[1] // TILE
    first_block, odd = info_ref[META, 0], info_ref[META, 1]
    parts, ones = [], []
    for j in range(NBT):
        local = info_ref[j, b] - first_block
        lower, upper = local < 0, local >= blocks
        at = lanes(jnp.where(lower, local + blocks, jnp.where(upper, local - blocks, local)))
        used = j < info_ref[COUNTS, b]
        x = own_ref[:, at]
        if j > 0:
            near = jnp.logical_or(jnp.logical_and(lower, odd == 1), jnp.logical_and(upper, odd == 0))
            beside = jnp.where(near, pair_ref[:, at], other_ref[:, at])
            x = beside if j < 3 else jnp.where(jnp.logical_or(lower, upper), beside, x)
        if j >= 3:
            x = jnp.where(used, x, jnp.zeros_like(x))
        parts.append(x)
        ones.append(jnp.full((16, TILE), jnp.where(used, 1.0, 0.0), jnp.float32).astype(jnp.bfloat16))
    lhs = jnp.concatenate(parts, axis=1)
    if with_degree:
        lhs = jnp.concatenate([lhs, jnp.concatenate(ones, axis=1)], axis=0)
    return dot_last(lhs, jnp.concatenate([tiles_ref[b, j] for j in range(NBT)], axis=1))


def first_kernel(info_ref, tiles_ref, own_ref, other_ref, pair_ref, out_ref, inv_ref):
    feats = own_ref.shape[0]
    for b in range(tiles_ref.shape[0]):
        out = step_block(info_ref, tiles_ref, own_ref, pair_ref, other_ref, b, True)
        inv = 1.0 / out[feats:feats + 8]
        inv_ref[b] = inv
        out_ref[:, b * TILE:(b + 1) * TILE] = (out[:feats] * inv[:1]).astype(jnp.bfloat16)


def second_kernel(info_ref, tiles_ref, own_ref, other_ref, pair_ref, inv_ref, extra_ref, out_ref):
    for b in range(tiles_ref.shape[0]):
        out = step_block(info_ref, tiles_ref, own_ref, pair_ref, other_ref, b, False)
        out_ref[:, b * TILE:(b + 1) * TILE] = (out * inv_ref[b][:1]).astype(jnp.bfloat16)


def arch_kernel(info_ref, table_ref, r0, r1, r2, r3, v_ref, out_ref):
    blocks = v_ref.shape[1] // TILE
    narch = r0.shape[0]
    me = info_ref[META, 2]
    block = lax.div(column(table_ref[ARCH:ARCH + 1, :narch], narch), TILE) - info_ref[META, 0]
    offsets = r0[:, 2 * TILE:].astype(jnp.float32)
    lane = lax.broadcasted_iota(jnp.int32, offsets.shape, 1)
    rows, places = [], []
    for p, r in enumerate((r0, r1, r2, r3)):
        for i in range(2):
            rows.append(r[:, i * TILE:(i + 1) * TILE].astype(jnp.float32))
            here = jnp.where(lane == 2 * (me ^ p) + i, offsets, 0.0)
            places.append(jnp.sum(here, axis=1, keepdims=True).astype(jnp.int32) + block)
    degree = jnp.sum(sum(rows), axis=1, keepdims=True)
    inv = jnp.where(degree > 0.0, 1.0 / degree, 0.0)
    rows = [r * inv for r in rows]
    weights = []
    for b in range(blocks):
        w = jnp.zeros((narch, TILE), jnp.float32)
        for r, place in zip(rows, places):
            w = w + jnp.where(place == b, r, 0.0)
        weights.append(jnp.concatenate(halves(w), axis=0))
    both = dot_last(jnp.concatenate(weights, axis=1), v_ref[...])
    part = both[:narch] + both[narch:]
    half = narch // 2
    out_ref[...] = jnp.concatenate([part[:half], part[half:]], axis=1)


def splat(x, shape):
    return jnp.broadcast_to(x, shape)


def solve_kernel(info_ref, total_ref, d0, d1, d2, d3, out_ref, copy_ref, whole_ref, scale_ref):
    total = total_ref[...].astype(jnp.bfloat16)
    feats, width = d0.shape
    n = total.shape[0] // 2
    copy_ref[...] = d0[...]
    step = 256
    for c in range(0, width, step):
        d = jnp.concatenate(in_order(info_ref[META, 2], [d[:, c:c + step] for d in (d0, d1, d2, d3)]), axis=0)
        whole_ref[:, c:c + step] = d
        wide = d.astype(jnp.float32)
        scale_ref[:, c:c + step] = lax.rsqrt(jnp.sum(wide * wide, axis=0, keepdims=True) / F + EPS)
    part = n // 2
    pieces = [total[p * part:(p + 1) * part] for p in range(4)]
    pieces = [jnp.concatenate([p[:, :feats], p[:, feats:]], axis=0) for p in pieces]
    pieces = in_order(info_ref[META, 2], pieces)
    arch = jnp.concatenate(pieces, axis=1)
    shape = (n, TILE)
    row = lax.broadcasted_iota(jnp.int32, shape, 0)
    col = lax.broadcasted_iota(jnp.int32, shape, 1)
    aug = jnp.concatenate([dot_last(arch, arch), jnp.zeros((n, TILE - n), jnp.float32)], axis=1)
    aug = aug + jnp.where(row + n == col, 1.0, 0.0)
    diagonal = jnp.zeros(shape, jnp.float32)
    group = 8
    for start in range(0, n, group):
        columns = [splat(aug[:, start + m:start + m + 1], shape) for m in range(group)]
        for m in range(group):
            k = start + m
            pivot = splat(columns[m][k:k + 1], shape)
            diagonal = jnp.where(row == k, pivot, diagonal)
            factor = jnp.where(row > k, columns[m] * (1.0 / pivot), 0.0)
            for later in range(m + 1, group):
                columns[later] = columns[later] - factor * splat(columns[later][k:k + 1], shape)
            aug = aug - factor * splat(aug[k:k + 1], shape)
    inverse = aug[:, n:2 * n] / jnp.sqrt(diagonal[:, :n])
    high, low = halves(inverse)
    third = (inverse - high.astype(jnp.float32) - low.astype(jnp.float32)).astype(jnp.bfloat16)
    q = dot(jnp.concatenate([high, low, third], axis=0), arch)
    q = jnp.concatenate(halves(q[:n] + q[n:2 * n] + q[2 * n:]), axis=0)
    for c in range(0, width, step):
        z = dot(q, whole_ref[:, c:c + step])
        out_ref[:, c:c + step] = (z[:n] + z[n:]) * scale_ref[:, c:c + step]


def in_order(me, pieces):
    for bit in (1, 2):
        flip = (me & bit) == bit
        pieces = [jnp.where(flip, pieces[i ^ bit], pieces[i]) for i in range(4)]
    return pieces


def call(kernel, out_shape, kinds, args, flops, nbytes, scratch=(), limit=16):
    single = not isinstance(out_shape, (list, tuple))
    spec = {"s": SMEM, "v": VMEM, "a": ANY, "h": HBM}
    return pl.pallas_call(
        kernel,
        out_shape=out_shape,
        in_specs=[spec[k] for k in kinds],
        out_specs=VMEM if single else [VMEM] * len(out_shape),
        scratch_shapes=scratch,
        compiler_params=pltpu.CompilerParams(vmem_limit_bytes=limit << 20),
        cost_estimate=pl.CostEstimate(flops=flops, bytes_accessed=nbytes, transcendentals=0),
    )(*args)


def exchange(matrix):
    size = lax.axis_size("cells")
    pairs = [(i, i ^ 1) for i in range(size)]
    others = [(i, i + 1) for i in range(1, size - 1, 2)]
    others = others + [(j, i) for i, j in others]
    return lax.ppermute(matrix, "cells", pairs), lax.ppermute(matrix, "cells", others)


def flip_feat(x, bits):
    return lax.ppermute(x, "feat", [(i, i ^ bits) for i in range(lax.axis_size("feat"))])


def on_device(expression, tiles, tile_cols, tile_counts, archetypes):
    blocks = tiles.shape[0]
    feats, rows = expression.shape
    narch = archetypes.shape[0]
    size = lax.axis_size("cells")
    cell, feat = lax.axis_index("cells"), lax.axis_index("feat")
    shape = jax.ShapeDtypeStruct
    bf16, f32 = jnp.bfloat16, jnp.float32
    line = lambda x: jnp.pad(x, ((0, 0), (0, TILE - x.shape[1])))
    numbers = jnp.stack([cell * blocks, cell & 1, feat]).astype(jnp.int32)
    info = jnp.concatenate([line(x) for x in (tile_cols.T, archetypes[None], tile_counts[None], numbers[None])], axis=0)
    flops = 2 * feats * TILE * TILE * NBT * blocks
    nbytes = 2 * TILE * TILE * NBT * blocks

    pair, other = exchange(expression)
    arch_rows, own = call(rows_kernel, [shape((narch, 3 * TILE), bf16), shape((feats, rows), bf16)], "svhh",
                     (info, info, tiles, expression), 0, 0,
                     [pltpu.VMEM((blocks, 2, TILE, TILE), bf16), pltpu.SemaphoreType.DMA((3,))], 52)
    first, inv = call(first_kernel, [shape((feats, rows), bf16), shape((blocks, 8, TILE), f32)], "svvvv",
                      (info, tiles, own, other, pair), flops, nbytes)

    row_pair, row_other = exchange(arch_rows)
    own_rows, _ = lax.optimization_barrier((arch_rows, other))
    near_rows, _ = lax.optimization_barrier((own_rows + row_pair + row_other, first))
    r = [near_rows] + [flip_feat(near_rows[:, :2 * TILE], p) for p in (1, 2, 3)]
    pair, other = exchange(first)
    part = call(arch_kernel, shape((narch // 2, 2 * feats), f32), "svvvvvv", (info, info, *r, first), 0, 0)
    step = (info, tiles, first, other, pair, inv)
    diffused = call(second_kernel, shape((feats, rows), bf16), "svvvvva", (*step, part), flops * 16, 0)
    seen, diffused = lax.optimization_barrier(([flip_feat(part, p) for p in (1, 2, 3)], diffused))
    part = jnp.concatenate([part, *seen], axis=0)
    flip_cells = lambda x, bits: lax.ppermute(x, "cells", [(i, i ^ bits) for i in range(size)])
    levels = (size - 1).bit_length()
    level = levels % 2
    if level:
        part = part + flip_cells(part, 1)

    pieces = [diffused, flip_feat(diffused, 1), flip_feat(diffused, 2)]
    pieces.append(flip_feat(pieces[2], 1))
    while level < levels:
        near, far, both = (flip_cells(part, b << level) for b in (1, 2, 3))
        part = (part + near) + (far + both)
        level += 2
    coords, diffused = call(
        solve_kernel, [shape((narch, rows), f32), shape((feats, rows), bf16)], "svvvvv",
        (info, part, *pieces), 4 * narch * F * rows, 4 * narch * rows,
        [pltpu.VMEM((4 * feats, rows), bf16), pltpu.VMEM((1, rows), f32)])
    return diffused, coords


def solution(mesh):
    return jax.shard_map(
        on_device,
        mesh=mesh,
        in_specs=(
            P("feat", "cells"),
            P("cells", None, None, None),
            P("cells", None),
            P("cells"),
            P(),
        ),
        out_specs=(P("feat", "cells"), P(None, "cells")),
        check_vma=False,
    )
```

```python
import functools
import jax
import jax.numpy as jnp
from jax import lax
from jax.experimental import pallas as pl
from jax.experimental.pallas import tpu as pltpu
from jax.sharding import PartitionSpec as P

F = 256
TILE = 128
NBT = 8
EPS = 1e-05
ARCH, COUNTS, META = range(NBT, NBT + 3)
OWN, PAIR, OTHER = range(1, 4)

VMEM = pl.BlockSpec(memory_space=pltpu.VMEM)
ANY = pl.BlockSpec(memory_space=pl.ANY)
HBM = pl.BlockSpec(memory_space=pltpu.HBM)


def dot_last(a, b):
    return lax.dot_general(a, b, (((1,), (1,)), ((), ())), preferred_element_type=jnp.float32)


def dot(a, b):
    return lax.dot_general(a, b, (((1,), (0,)), ((), ())), preferred_element_type=jnp.float32)


def lanes(block):
    return pl.ds(pl.multiple_of(block * TILE, TILE), TILE)


def wide_tile(tiles_ref, b, slots):
    return jnp.concatenate([tiles_ref[b, j] for j in slots], axis=1)


def halves(x):
    high = x.astype(jnp.bfloat16)
    return high, (x - high.astype(jnp.float32)).astype(jnp.bfloat16)


def column(row, narch):
    at = lax.broadcasted_iota(jnp.int32, (narch, narch), 0) == lax.broadcasted_iota(jnp.int32, (narch, narch), 1)
    return jnp.sum(jnp.where(at, row.astype(jnp.float32), 0.0), axis=1, keepdims=True).astype(jnp.int32)


def rows_kernel(info_ref, table_ref, tiles_ref, v_ref, rows_ref, own_ref, held_ref, sem):
    blocks = tiles_ref.shape[0]
    narch = rows_ref.shape[0]
    info = info_ref[...]
    first_block, first_slot = info[META, 0], 2 * info[META, 2]
    whole = pltpu.make_async_copy(v_ref, own_ref, sem.at[2])
    whole.start()
    copies = []
    for i in range(2):
        copies.append(pltpu.make_async_copy(tiles_ref.at[:, first_slot + i], held_ref.at[:, i], sem.at[i]))
        copies[-1].start()
    local = column(table_ref[ARCH:ARCH + 1, :narch], narch) - first_block * TILE
    at = lax.broadcasted_iota(jnp.int32, (narch, TILE), 1)
    hits = [(local - b * TILE) == at for b in range(blocks)]
    owner = lax.broadcasted_iota(jnp.int32, (narch, blocks), 1) == lax.div(local, TILE)
    owner = jnp.where(jnp.logical_and(owner, local >= 0), 1.0, 0.0).astype(jnp.bfloat16)
    cols = table_ref[:NBT, :blocks]
    steps = cols - first_block - lax.broadcasted_iota(jnp.int32, cols.shape, 1)
    steps = dot_last(owner, steps.astype(jnp.float32).astype(jnp.bfloat16))
    rows_ref[:, 2 * TILE:] = jnp.zeros((narch, TILE), jnp.bfloat16)
    rows_ref[:, 2 * TILE:2 * TILE + NBT] = steps.astype(jnp.bfloat16)
    for i in range(2):
        sel = [
            jnp.where(hit, jnp.where(first_slot + i < info[COUNTS, b], 1.0, 0.0), 0.0).astype(jnp.bfloat16)
            for b, hit in enumerate(hits)
        ]
        copies[i].wait()
        tall = jnp.concatenate([held_ref[b, i] for b in range(blocks)], axis=0)
        row = dot(jnp.concatenate(sel, axis=1), tall)
        rows_ref[:, i * TILE:(i + 1) * TILE] = row.astype(jnp.bfloat16)
    whole.wait()


def slot_codes(info_ref, blocks):
    shape = (NBT, TILE)
    local = info_ref[:NBT] - info_ref[META:META + 1, :1]
    odd = jnp.broadcast_to(info_ref[META:META + 1, 1:2], shape)
    counts = jnp.broadcast_to(info_ref[COUNTS:COUNTS + 1], shape)
    below = jnp.where(odd == 1, PAIR, OTHER)
    side = jnp.where(local < 0, below, jnp.where(local >= blocks, PAIR + OTHER - below, OWN))
    at = jnp.where(local < 0, local + blocks, jnp.where(local >= blocks, local - blocks, local))
    used = lax.broadcasted_iota(jnp.int32, shape, 0) < counts
    return jnp.where(used, side, 0) * blocks + at


def step_block(codes, tiles_ref, own_ref, pair_ref, other_ref, b, with_degree):
    blocks = tiles_ref.shape[0]
    parts, ones = [], []
    for j in range(NBT):
        code = codes[j, b]
        side, at = lax.div(code, blocks), lanes(lax.rem(code, blocks))
        x = own_ref[:, at]
        if j > 0:
            beside = jnp.where(side == PAIR, pair_ref[:, at], other_ref[:, at])
            x = beside if j < 3 else jnp.where(side == OWN, x, beside)
        if j >= 3:
            x = jnp.where(side > 0, x, jnp.zeros_like(x))
        parts.append(x)
        ones.append(jnp.full((16, TILE), jnp.where(side > 0, 1.0, 0.0), jnp.float32).astype(jnp.bfloat16))
    lhs = jnp.concatenate(parts, axis=1)
    if with_degree:
        lhs = jnp.concatenate([lhs, jnp.concatenate(ones, axis=1)], axis=0)
    return dot_last(lhs, jnp.concatenate([tiles_ref[b, j] for j in range(NBT)], axis=1))


def first_kernel(info_ref, tiles_ref, own_ref, other_ref, pair_ref, out_ref, inv_ref):
    feats = own_ref.shape[0]
    codes = slot_codes(info_ref, tiles_ref.shape[0])
    for b in range(tiles_ref.shape[0]):
        out = step_block(codes, tiles_ref, own_ref, pair_ref, other_ref, b, True)
        inv = 1.0 / out[feats:feats + 8]
        inv_ref[b] = inv
        out_ref[:, b * TILE:(b + 1) * TILE] = (out[:feats] * inv[:1]).astype(jnp.bfloat16)


def second_kernel(info_ref, tiles_ref, own_ref, other_ref, pair_ref, inv_ref, extra_ref, out_ref):
    codes = slot_codes(info_ref, tiles_ref.shape[0])
    for b in range(tiles_ref.shape[0]):
        out = step_block(codes, tiles_ref, own_ref, pair_ref, other_ref, b, False)
        out_ref[:, b * TILE:(b + 1) * TILE] = (out * inv_ref[b][:1]).astype(jnp.bfloat16)


def arch_kernel(info_ref, table_ref, r0, r1, r2, r3, v_ref, out_ref):
    blocks = v_ref.shape[1] // TILE
    narch = r0.shape[0]
    info = info_ref[...]
    me = info[META, 2]
    block = lax.div(column(table_ref[ARCH:ARCH + 1, :narch], narch), TILE) - info[META, 0]
    offsets = r0[:, 2 * TILE:].astype(jnp.float32)
    lane = lax.broadcasted_iota(jnp.int32, offsets.shape, 1)
    rows, places = [], []
    for p, r in enumerate((r0, r1, r2, r3)):
        for i in range(2):
            rows.append(r[:, i * TILE:(i + 1) * TILE].astype(jnp.float32))
            here = jnp.where(lane == 2 * (me ^ p) + i, offsets, 0.0)
            places.append(jnp.sum(here, axis=1, keepdims=True).astype(jnp.int32) + block)
    degree = jnp.sum(sum(rows), axis=1, keepdims=True)
    inv = jnp.where(degree > 0.0, 1.0 / degree, 0.0)
    rows = [r * inv for r in rows]
    weights = []
    for b in range(blocks):
        w = jnp.zeros((narch, TILE), jnp.float32)
        for r, place in zip(rows, places):
            w = w + jnp.where(place == b, r, 0.0)
        weights.append(jnp.concatenate(halves(w), axis=0))
    both = dot_last(jnp.concatenate(weights, axis=1), v_ref[...])
    part = both[:narch] + both[narch:]
    half = narch // 2
    out_ref[...] = jnp.concatenate([part[:half], part[half:]], axis=1)


def splat(x, shape):
    return jnp.broadcast_to(x, shape)


def solve_kernel(info_ref, total_ref, d0, d1, d2, d3, out_ref, copy_ref, whole_ref, scale_ref, made_ref, sem):
    total = total_ref[...].astype(jnp.bfloat16)
    feats, width = d0.shape
    n = total.shape[0] // 2
    same = pltpu.make_async_copy(d0, copy_ref, sem.at[0])
    same.start()
    me = info_ref[...][META, 2]
    step = 256
    for c in range(0, width, step):
        d = jnp.concatenate(in_order(me, [d[:, c:c + step] for d in (d0, d1, d2, d3)]), axis=0)
        whole_ref[:, c:c + step] = d
        wide = d.astype(jnp.float32)
        scale_ref[:, c:c + step] = lax.rsqrt(jnp.sum(wide * wide, axis=0, keepdims=True) / F + EPS)
    part = n // 2
    pieces = [total[p * part:(p + 1) * part] for p in range(4)]
    pieces = [jnp.concatenate([p[:, :feats], p[:, feats:]], axis=0) for p in pieces]
    pieces = in_order(me, pieces)
    arch = jnp.concatenate(pieces, axis=1)
    shape = (n, TILE)
    row = lax.broadcasted_iota(jnp.int32, shape, 0)
    col = lax.broadcasted_iota(jnp.int32, shape, 1)
    aug = jnp.concatenate([dot_last(arch, arch), jnp.zeros((n, TILE - n), jnp.float32)], axis=1)
    aug = aug + jnp.where(row + n == col, 1.0, 0.0)
    diagonal = jnp.zeros(shape, jnp.float32)
    group = 8
    for start in range(0, n, group):
        columns = [splat(aug[:, start + m:start + m + 1], shape) for m in range(group)]
        for m in range(group):
            k = start + m
            pivot = splat(columns[m][k:k + 1], shape)
            diagonal = jnp.where(row == k, pivot, diagonal)
            factor = jnp.where(row > k, columns[m] * (1.0 / pivot), 0.0)
            for later in range(m + 1, group):
                columns[later] = columns[later] - factor * splat(columns[later][k:k + 1], shape)
            aug = aug - factor * splat(aug[k:k + 1], shape)
    inverse = aug[:, n:2 * n] / jnp.sqrt(diagonal[:, :n])
    high, low = halves(inverse)
    third = (inverse - high.astype(jnp.float32) - low.astype(jnp.float32)).astype(jnp.bfloat16)
    q = dot(jnp.concatenate([high, low, third], axis=0), arch)
    q = jnp.concatenate(halves(q[:n] + q[n:2 * n] + q[2 * n:]), axis=0)
    copies = [same]
    for i, c in enumerate(range(0, width, step)):
        z = dot(q, whole_ref[:, c:c + step])
        made_ref[:, c:c + step] = (z[:n] + z[n:]) * scale_ref[:, c:c + step]
        copies.append(pltpu.make_async_copy(made_ref.at[:, c:c + step], out_ref.at[:, c:c + step], sem.at[1 + i]))
        copies[-1].start()
    for copy in copies:
        copy.wait()


def in_order(me, pieces):
    for bit in (1, 2):
        flip = (me & bit) == bit
        pieces = [jnp.where(flip, pieces[i ^ bit], pieces[i]) for i in range(4)]
    return pieces


def call(kernel, out_shape, kinds, args, flops, nbytes, scratch=(), limit=16, place=VMEM):
    single = not isinstance(out_shape, (list, tuple))
    spec = {"v": VMEM, "a": ANY, "h": HBM}
    return pl.pallas_call(
        kernel,
        out_shape=out_shape,
        in_specs=[spec[k] for k in kinds],
        out_specs=place if single else [place] * len(out_shape),
        scratch_shapes=scratch,
        compiler_params=pltpu.CompilerParams(vmem_limit_bytes=limit << 20),
        cost_estimate=pl.CostEstimate(flops=flops, bytes_accessed=nbytes, transcendentals=0),
    )(*args)


def exchange(matrix):
    size = lax.axis_size("cells")
    pairs = [(i, i ^ 1) for i in range(size)]
    others = [(i, i + 1) for i in range(1, size - 1, 2)]
    others = others + [(j, i) for i, j in others]
    return lax.ppermute(matrix, "cells", pairs), lax.ppermute(matrix, "cells", others)


def flip_feat(x, bits):
    return lax.ppermute(x, "feat", [(i, i ^ bits) for i in range(lax.axis_size("feat"))])


def on_device(expression, tiles, tile_cols, tile_counts, archetypes):
    blocks = tiles.shape[0]
    feats, rows = expression.shape
    narch = archetypes.shape[0]
    size = lax.axis_size("cells")
    cell, feat = lax.axis_index("cells"), lax.axis_index("feat")
    shape = jax.ShapeDtypeStruct
    bf16, f32 = jnp.bfloat16, jnp.float32
    line = lambda x: jnp.pad(x, ((0, 0), (0, TILE - x.shape[1])))
    numbers = jnp.stack([cell * blocks, cell & 1, feat]).astype(jnp.int32)
    info = jnp.concatenate([line(x) for x in (tile_cols.T, archetypes[None], tile_counts[None], numbers[None])], axis=0)
    flops = 2 * feats * TILE * TILE * NBT * blocks
    nbytes = 2 * TILE * TILE * NBT * blocks

    pair, other = exchange(expression)
    arch_rows, own = call(rows_kernel, [shape((narch, 3 * TILE), bf16), shape((feats, rows), bf16)], "vvhh",
                     (info, info, tiles, expression), 0, 0,
                     [pltpu.VMEM((blocks, 2, TILE, TILE), bf16), pltpu.SemaphoreType.DMA((3,))], 52)
    first, inv = call(first_kernel, [shape((feats, rows), bf16), shape((blocks, 8, TILE), f32)], "vvvvv",
                      (info, tiles, own, other, pair), flops, nbytes)

    row_pair, row_other = exchange(arch_rows)
    own_rows, _ = lax.optimization_barrier((arch_rows, other))
    near_rows, _ = lax.optimization_barrier((own_rows + row_pair + row_other, first))
    r = [near_rows] + [flip_feat(near_rows[:, :2 * TILE], p) for p in (1, 2, 3)]
    pair, other = exchange(first)
    part = call(arch_kernel, shape((narch // 2, 2 * feats), f32), "vvvvvvv", (info, info, *r, first), 0, 0)
    step = (info, tiles, first, other, pair, inv)
    diffused = call(second_kernel, shape((feats, rows), bf16), "vvvvvva", (*step, part), flops * 16, 0)
    seen, diffused = lax.optimization_barrier(([flip_feat(part, p) for p in (1, 2, 3)], diffused))
    part = jnp.concatenate([part, *seen], axis=0)
    flip_cells = lambda x, bits: lax.ppermute(x, "cells", [(i, i ^ bits) for i in range(size)])
    levels = (size - 1).bit_length()
    level = levels % 2
    if level:
        part = part + flip_cells(part, 1)

    pieces = [diffused, flip_feat(diffused, 1), flip_feat(diffused, 2)]
    pieces.append(flip_feat(pieces[2], 1))
    while level < levels:
        near, far, both = (flip_cells(part, b << level) for b in (1, 2, 3))
        part = (part + near) + (far + both)
        level += 2
    coords, diffused = call(
        solve_kernel, [shape((narch, rows), f32), shape((feats, rows), bf16)], "vvvvvv",
        (info, part, *pieces), 4 * narch * F * rows, 4 * narch * rows,
        [pltpu.VMEM((4 * feats, rows), bf16), pltpu.VMEM((1, rows), f32), pltpu.VMEM((narch, rows), f32),
         pltpu.SemaphoreType.DMA((1 + rows // 256,))], place=HBM)
    return diffused, coords


def solution(mesh):
    return jax.shard_map(
        on_device,
        mesh=mesh,
        in_specs=(
            P("feat", "cells"),
            P("cells", None, None, None),
            P("cells", None),
            P("cells"),
            P(),
        ),
        out_specs=(P("feat", "cells"), P(None, "cells")),
        check_vma=False,
    )
```

```python
import functools
import jax
import jax.numpy as jnp
from jax import lax
from jax.experimental import pallas as pl
from jax.experimental.pallas import tpu as pltpu
from jax.sharding import PartitionSpec as P

F = 256
TILE = 128
NBT = 8
EPS = 1e-05
ARCH, COUNTS, META = range(NBT, NBT + 3)
OWN, PAIR, OTHER = range(1, 4)

VMEM = pl.BlockSpec(memory_space=pltpu.VMEM)
ANY = pl.BlockSpec(memory_space=pl.ANY)
HBM = pl.BlockSpec(memory_space=pltpu.HBM)


def dot_last(a, b):
    return lax.dot_general(a, b, (((1,), (1,)), ((), ())), preferred_element_type=jnp.float32)


def dot(a, b):
    return lax.dot_general(a, b, (((1,), (0,)), ((), ())), preferred_element_type=jnp.float32)


def lanes(block):
    return pl.ds(pl.multiple_of(block * TILE, TILE), TILE)


def wide_tile(tiles_ref, b, slots):
    return jnp.concatenate([tiles_ref[b, j] for j in slots], axis=1)


def halves(x):
    high = x.astype(jnp.bfloat16)
    return high, (x - high.astype(jnp.float32)).astype(jnp.bfloat16)


def column(row, narch):
    at = lax.broadcasted_iota(jnp.int32, (narch, narch), 0) == lax.broadcasted_iota(jnp.int32, (narch, narch), 1)
    return jnp.sum(jnp.where(at, row.astype(jnp.float32), 0.0), axis=1, keepdims=True).astype(jnp.int32)


def rows_kernel(info_ref, table_ref, tiles_ref, v_ref, rows_ref, own_ref, held_ref, sem):
    blocks = tiles_ref.shape[0]
    narch = rows_ref.shape[0]
    info = info_ref[...]
    first_block, first_slot = info[META, 0], 2 * info[META, 2]
    whole = pltpu.make_async_copy(v_ref, own_ref, sem.at[2])
    whole.start()
    copies = []
    for i in range(2):
        copies.append(pltpu.make_async_copy(tiles_ref.at[:, first_slot + i], held_ref.at[:, i], sem.at[i]))
        copies[-1].start()
    local = column(table_ref[ARCH:ARCH + 1, :narch], narch) - first_block * TILE
    at = lax.broadcasted_iota(jnp.int32, (narch, TILE), 1)
    hits = [(local - b * TILE) == at for b in range(blocks)]
    owner = lax.broadcasted_iota(jnp.int32, (narch, blocks), 1) == lax.div(local, TILE)
    owner = jnp.where(jnp.logical_and(owner, local >= 0), 1.0, 0.0).astype(jnp.bfloat16)
    cols = table_ref[:NBT, :blocks]
    steps = cols - first_block - lax.broadcasted_iota(jnp.int32, cols.shape, 1)
    steps = dot_last(owner, steps.astype(jnp.float32).astype(jnp.bfloat16))
    rows_ref[:, 2 * TILE:] = jnp.zeros((narch, TILE), jnp.bfloat16)
    rows_ref[:, 2 * TILE:2 * TILE + NBT] = steps.astype(jnp.bfloat16)
    for i in range(2):
        sel = [
            jnp.where(hit, jnp.where(first_slot + i < info[COUNTS, b], 1.0, 0.0), 0.0).astype(jnp.bfloat16)
            for b, hit in enumerate(hits)
        ]
        copies[i].wait()
        tall = jnp.concatenate([held_ref[b, i] for b in range(blocks)], axis=0)
        row = dot(jnp.concatenate(sel, axis=1), tall)
        rows_ref[:, i * TILE:(i + 1) * TILE] = row.astype(jnp.bfloat16)
    whole.wait()


def slot_codes(info_ref, blocks):
    shape = (NBT, TILE)
    local = info_ref[:NBT] - info_ref[META:META + 1, :1]
    odd = jnp.broadcast_to(info_ref[META:META + 1, 1:2], shape)
    counts = jnp.broadcast_to(info_ref[COUNTS:COUNTS + 1], shape)
    below = jnp.where(odd == 1, PAIR, OTHER)
    side = jnp.where(local < 0, below, jnp.where(local >= blocks, PAIR + OTHER - below, OWN))
    at = jnp.where(local < 0, local + blocks, jnp.where(local >= blocks, local - blocks, local))
    used = lax.broadcasted_iota(jnp.int32, shape, 0) < counts
    return jnp.where(used, side, 0) * blocks + at


def step_block(codes, tiles_ref, own_ref, pair_ref, other_ref, b, with_degree):
    blocks = tiles_ref.shape[0]
    parts, ones = [], []
    for j in range(NBT):
        code = codes[j, b]
        side, at = lax.div(code, blocks), lanes(lax.rem(code, blocks))
        x = own_ref[:, at]
        if j > 0:
            beside = jnp.where(side == PAIR, pair_ref[:, at], other_ref[:, at])
            x = beside if j < 3 else jnp.where(side == OWN, x, beside)
        if j >= 3:
            x = jnp.where(side > 0, x, jnp.zeros_like(x))
        parts.append(x)
        ones.append(jnp.full((16, TILE), jnp.where(side > 0, 1.0, 0.0), jnp.float32).astype(jnp.bfloat16))
    lhs = jnp.concatenate(parts, axis=1)
    if with_degree:
        lhs = jnp.concatenate([lhs, jnp.concatenate(ones, axis=1)], axis=0)
    return dot_last(lhs, jnp.concatenate([tiles_ref[b, j] for j in range(NBT)], axis=1))


def first_kernel(info_ref, tiles_ref, own_ref, other_ref, pair_ref, out_ref, inv_ref):
    feats = own_ref.shape[0]
    codes = slot_codes(info_ref, tiles_ref.shape[0])
    for b in range(tiles_ref.shape[0]):
        out = step_block(codes, tiles_ref, own_ref, pair_ref, other_ref, b, True)
        inv = 1.0 / out[feats:feats + 8]
        inv_ref[b] = inv
        out_ref[:, b * TILE:(b + 1) * TILE] = (out[:feats] * inv[:1]).astype(jnp.bfloat16)


def second_kernel(info_ref, tiles_ref, own_ref, other_ref, pair_ref, inv_ref, extra_ref, out_ref):
    codes = slot_codes(info_ref, tiles_ref.shape[0])
    for b in range(tiles_ref.shape[0]):
        out = step_block(codes, tiles_ref, own_ref, pair_ref, other_ref, b, False)
        out_ref[:, b * TILE:(b + 1) * TILE] = (out * inv_ref[b][:1]).astype(jnp.bfloat16)


def arch_kernel(info_ref, table_ref, r0, r1, r2, r3, v_ref, out_ref):
    blocks = v_ref.shape[1] // TILE
    narch = r0.shape[0]
    info = info_ref[...]
    me = info[META, 2]
    block = lax.div(column(table_ref[ARCH:ARCH + 1, :narch], narch), TILE) - info[META, 0]
    offsets = r0[:, 2 * TILE:].astype(jnp.float32)
    lane = lax.broadcasted_iota(jnp.int32, offsets.shape, 1)
    rows, places = [], []
    for p, r in enumerate((r0, r1, r2, r3)):
        for i in range(2):
            rows.append(r[:, i * TILE:(i + 1) * TILE].astype(jnp.float32))
            here = jnp.where(lane == 2 * (me ^ p) + i, offsets, 0.0)
            places.append(jnp.sum(here, axis=1, keepdims=True).astype(jnp.int32) + block)
    degree = jnp.sum(sum(rows), axis=1, keepdims=True)
    inv = jnp.where(degree > 0.0, 1.0 / degree, 0.0)
    rows = [r * inv for r in rows]
    weights = []
    for b in range(blocks):
        w = jnp.zeros((narch, TILE), jnp.float32)
        for r, place in zip(rows, places):
            w = w + jnp.where(place == b, r, 0.0)
        weights.append(jnp.concatenate(halves(w), axis=0))
    both = dot_last(jnp.concatenate(weights, axis=1), v_ref[...])
    part = both[:narch] + both[narch:]
    half = narch // 2
    out_ref[...] = jnp.concatenate([part[:half], part[half:]], axis=1)


def splat(x, shape):
    return jnp.broadcast_to(x, shape)


def solve_kernel(info_ref, total_ref, d0, d1, d2, d3, out_ref, copy_ref, whole_ref, scale_ref, made_ref, sem):
    total = total_ref[...].astype(jnp.bfloat16)
    feats, width = d0.shape
    n = total.shape[0] // 2
    same = pltpu.make_async_copy(d0, copy_ref, sem.at[0])
    same.start()
    me = info_ref[...][META, 2]
    step = 256
    for c in range(0, width, step):
        d = jnp.concatenate(in_order(me, [d[:, c:c + step] for d in (d0, d1, d2, d3)]), axis=0)
        whole_ref[:, c:c + step] = d
        wide = d.astype(jnp.float32)
        scale_ref[:, c:c + step] = lax.rsqrt(jnp.sum(wide * wide, axis=0, keepdims=True) / F + EPS)
    part = n // 2
    pieces = [total[p * part:(p + 1) * part] for p in range(4)]
    pieces = [jnp.concatenate([p[:, :feats], p[:, feats:]], axis=0) for p in pieces]
    pieces = in_order(me, pieces)
    arch = jnp.concatenate(pieces, axis=1)
    shape = (n, TILE)
    row = lax.broadcasted_iota(jnp.int32, shape, 0)
    col = lax.broadcasted_iota(jnp.int32, shape, 1)
    aug = jnp.concatenate([dot_last(arch, arch), jnp.zeros((n, TILE - n), jnp.float32)], axis=1)
    aug = aug + jnp.where(row + n == col, 1.0, 0.0)
    diagonal = jnp.zeros(shape, jnp.float32)
    group = 16
    for start in range(0, n, group):
        columns = [splat(aug[:, start + m:start + m + 1], shape) for m in range(group)]
        for m in range(group):
            k = start + m
            pivot = splat(columns[m][k:k + 1], shape)
            diagonal = jnp.where(row == k, pivot, diagonal)
            factor = jnp.where(row > k, columns[m] * (1.0 / pivot), 0.0)
            for later in range(m + 1, group):
                columns[later] = columns[later] - factor * splat(columns[later][k:k + 1], shape)
            aug = aug - factor * splat(aug[k:k + 1], shape)
    inverse = aug[:, n:2 * n] / jnp.sqrt(diagonal[:, :n])
    high, low = halves(inverse)
    third = (inverse - high.astype(jnp.float32) - low.astype(jnp.float32)).astype(jnp.bfloat16)
    q = dot(jnp.concatenate([high, low, third], axis=0), arch)
    q = jnp.concatenate(halves(q[:n] + q[n:2 * n] + q[2 * n:]), axis=0)
    copies = [same]
    for i, c in enumerate(range(0, width, step)):
        z = dot(q, whole_ref[:, c:c + step])
        made_ref[:, c:c + step] = (z[:n] + z[n:]) * scale_ref[:, c:c + step]
        copies.append(pltpu.make_async_copy(made_ref.at[:, c:c + step], out_ref.at[:, c:c + step], sem.at[1 + i]))
        copies[-1].start()
    for copy in copies:
        copy.wait()


def in_order(me, pieces):
    for bit in (1, 2):
        flip = (me & bit) == bit
        pieces = [jnp.where(flip, pieces[i ^ bit], pieces[i]) for i in range(4)]
    return pieces


def call(kernel, out_shape, kinds, args, flops, nbytes, scratch=(), limit=16, place=VMEM):
    single = not isinstance(out_shape, (list, tuple))
    spec = {"v": VMEM, "a": ANY, "h": HBM}
    return pl.pallas_call(
        kernel,
        out_shape=out_shape,
        in_specs=[spec[k] for k in kinds],
        out_specs=place if single else [place] * len(out_shape),
        scratch_shapes=scratch,
        compiler_params=pltpu.CompilerParams(vmem_limit_bytes=limit << 20),
        cost_estimate=pl.CostEstimate(flops=flops, bytes_accessed=nbytes, transcendentals=0),
    )(*args)


def exchange(matrix):
    size = lax.axis_size("cells")
    pairs = [(i, i ^ 1) for i in range(size)]
    others = [(i, i + 1) for i in range(1, size - 1, 2)]
    others = others + [(j, i) for i, j in others]
    return lax.ppermute(matrix, "cells", pairs), lax.ppermute(matrix, "cells", others)


def flip_feat(x, bits):
    return lax.ppermute(x, "feat", [(i, i ^ bits) for i in range(lax.axis_size("feat"))])


def on_device(expression, tiles, tile_cols, tile_counts, archetypes):
    blocks = tiles.shape[0]
    feats, rows = expression.shape
    narch = archetypes.shape[0]
    size = lax.axis_size("cells")
    cell, feat = lax.axis_index("cells"), lax.axis_index("feat")
    shape = jax.ShapeDtypeStruct
    bf16, f32 = jnp.bfloat16, jnp.float32
    line = lambda x: jnp.pad(x, ((0, 0), (0, TILE - x.shape[1])))
    numbers = jnp.stack([cell * blocks, cell & 1, feat]).astype(jnp.int32)
    info = jnp.concatenate([line(x) for x in (tile_cols.T, archetypes[None], tile_counts[None], numbers[None])], axis=0)
    flops = 2 * feats * TILE * TILE * NBT * blocks
    nbytes = 2 * TILE * TILE * NBT * blocks

    pair, other = exchange(expression)
    arch_rows, own = call(rows_kernel, [shape((narch, 3 * TILE), bf16), shape((feats, rows), bf16)], "vvhh",
                     (info, info, tiles, expression), 0, 0,
                     [pltpu.VMEM((blocks, 2, TILE, TILE), bf16), pltpu.SemaphoreType.DMA((3,))], 52)
    first, inv = call(first_kernel, [shape((feats, rows), bf16), shape((blocks, 8, TILE), f32)], "vvvvv",
                      (info, tiles, own, other, pair), flops, nbytes)

    row_pair, row_other = exchange(arch_rows)
    own_rows, _ = lax.optimization_barrier((arch_rows, other))
    near_rows, _ = lax.optimization_barrier((own_rows + row_pair + row_other, first))
    r = [near_rows] + [flip_feat(near_rows[:, :2 * TILE], p) for p in (1, 2, 3)]
    pair, other = exchange(first)
    part = call(arch_kernel, shape((narch // 2, 2 * feats), f32), "vvvvvvv", (info, info, *r, first), 0, 0)
    step = (info, tiles, first, other, pair, inv)
    diffused = call(second_kernel, shape((feats, rows), bf16), "vvvvvva", (*step, part), flops * 16, 0)
    seen, diffused = lax.optimization_barrier(([flip_feat(part, p) for p in (1, 2, 3)], diffused))
    part = jnp.concatenate([part, *seen], axis=0)
    flip_cells = lambda x, bits: lax.ppermute(x, "cells", [(i, i ^ bits) for i in range(size)])
    levels = (size - 1).bit_length()
    level = levels % 2
    if level:
        part = part + flip_cells(part, 1)

    pieces = [diffused, flip_feat(diffused, 1), flip_feat(diffused, 2)]
    pieces.append(flip_feat(pieces[2], 1))
    while level < levels:
        near, far, both = (flip_cells(part, b << level) for b in (1, 2, 3))
        part = (part + near) + (far + both)
        level += 2
    coords, diffused = call(
        solve_kernel, [shape((narch, rows), f32), shape((feats, rows), bf16)], "vvvvvv",
        (info, part, *pieces), 4 * narch * F * rows, 4 * narch * rows,
        [pltpu.VMEM((4 * feats, rows), bf16), pltpu.VMEM((1, rows), f32), pltpu.VMEM((narch, rows), f32),
         pltpu.SemaphoreType.DMA((1 + rows // 256,))], place=HBM)
    return diffused, coords


def solution(mesh):
    return jax.shard_map(
        on_device,
        mesh=mesh,
        in_specs=(
            P("feat", "cells"),
            P("cells", None, None, None),
            P("cells", None),
            P("cells"),
            P(),
        ),
        out_specs=(P("feat", "cells"), P(None, "cells")),
        check_vma=False,
    )
```

```python
import functools
import jax
import jax.numpy as jnp
from jax import lax
from jax.experimental import pallas as pl
from jax.experimental.pallas import tpu as pltpu
from jax.sharding import PartitionSpec as P

F = 256
TILE = 128
NBT = 8
EPS = 1e-05
ARCH, COUNTS, META = range(NBT, NBT + 3)

VMEM = pl.BlockSpec(memory_space=pltpu.VMEM)
ANY = pl.BlockSpec(memory_space=pl.ANY)
HBM = pl.BlockSpec(memory_space=pltpu.HBM)


def dot_last(a, b):
    return lax.dot_general(a, b, (((1,), (1,)), ((), ())), preferred_element_type=jnp.float32)


def dot(a, b):
    return lax.dot_general(a, b, (((1,), (0,)), ((), ())), preferred_element_type=jnp.float32)


def lanes(block):
    return pl.ds(pl.multiple_of(block * TILE, TILE), TILE)


def wide_tile(tiles_ref, b, slots):
    return jnp.concatenate([tiles_ref[b, j] for j in slots], axis=1)


def halves(x):
    high = x.astype(jnp.bfloat16)
    return high, (x - high.astype(jnp.float32)).astype(jnp.bfloat16)


def column(row, narch):
    at = lax.broadcasted_iota(jnp.int32, (narch, narch), 0) == lax.broadcasted_iota(jnp.int32, (narch, narch), 1)
    return jnp.sum(jnp.where(at, row.astype(jnp.float32), 0.0), axis=1, keepdims=True).astype(jnp.int32)


def rows_kernel(info_ref, table_ref, tiles_ref, v_ref, rows_ref, own_ref, held_ref, sem):
    blocks = tiles_ref.shape[0]
    narch = rows_ref.shape[0]
    info = info_ref[...]
    first_block, first_slot = info[META, 0], 2 * info[META, 2]
    whole = pltpu.make_async_copy(v_ref, own_ref, sem.at[2])
    whole.start()
    copies = []
    for i in range(2):
        copies.append(pltpu.make_async_copy(tiles_ref.at[:, first_slot + i], held_ref.at[:, i], sem.at[i]))
        copies[-1].start()
    local = column(table_ref[ARCH:ARCH + 1, :narch], narch) - first_block * TILE
    at = lax.broadcasted_iota(jnp.int32, (narch, TILE), 1)
    hits = [(local - b * TILE) == at for b in range(blocks)]
    owner = lax.broadcasted_iota(jnp.int32, (narch, blocks), 1) == lax.div(local, TILE)
    owner = jnp.where(jnp.logical_and(owner, local >= 0), 1.0, 0.0).astype(jnp.bfloat16)
    cols = table_ref[:NBT, :blocks]
    steps = cols - first_block - lax.broadcasted_iota(jnp.int32, cols.shape, 1)
    steps = dot_last(owner, steps.astype(jnp.float32).astype(jnp.bfloat16))
    rows_ref[:, 2 * TILE:] = jnp.zeros((narch, TILE), jnp.bfloat16)
    rows_ref[:, 2 * TILE:2 * TILE + NBT] = steps.astype(jnp.bfloat16)
    for i in range(2):
        sel = [
            jnp.where(hit, jnp.where(first_slot + i < info[COUNTS, b], 1.0, 0.0), 0.0).astype(jnp.bfloat16)
            for b, hit in enumerate(hits)
        ]
        copies[i].wait()
        tall = jnp.concatenate([held_ref[b, i] for b in range(blocks)], axis=0)
        row = dot(jnp.concatenate(sel, axis=1), tall)
        rows_ref[:, i * TILE:(i + 1) * TILE] = row.astype(jnp.bfloat16)
    whole.wait()


def slot_places(info_ref, blocks):
    shape = (NBT, TILE)
    local = info_ref[:NBT] - info_ref[META:META + 1, :1]
    odd = jnp.broadcast_to(info_ref[META:META + 1, 1:2], shape)
    counts = jnp.broadcast_to(info_ref[COUNTS:COUNTS + 1], shape)
    below = jnp.where(odd == 1, 1, 2)
    lower, upper = local + (below + 1) * blocks, local - blocks + (3 - below) * blocks
    at = jnp.where(local < 0, lower, jnp.where(local >= blocks, upper, local))
    used = lax.broadcasted_iota(jnp.int32, shape, 0) < counts
    return jnp.where(used, at, 3 * blocks)


def side_by_side(all_ref, own_ref, pair_ref, other_ref):
    width = own_ref.shape[1]
    for i, ref in enumerate((own_ref, pair_ref, other_ref)):
        all_ref[:, i * width:(i + 1) * width] = ref[...]
    all_ref[:, 3 * width:] = jnp.zeros_like(all_ref[:, 3 * width:])


def step_block(places, tiles_ref, own_ref, all_ref, b, with_degree):
    blocks = tiles_ref.shape[0]
    parts, ones = [], []
    for j in range(NBT):
        at = places[j, b]
        parts.append(all_ref[:, lanes(at)] if j else own_ref[:, b * TILE:(b + 1) * TILE])
        if with_degree:
            used = jnp.where(at < 3 * blocks, 1.0, 0.0)
            ones.append(jnp.full((16, TILE), used, jnp.float32).astype(jnp.bfloat16))
    lhs = jnp.concatenate(parts, axis=1)
    if with_degree:
        lhs = jnp.concatenate([lhs, jnp.concatenate(ones, axis=1)], axis=0)
    return dot_last(lhs, wide_tile(tiles_ref, b, range(NBT)))


def first_kernel(info_ref, tiles_ref, own_ref, other_ref, pair_ref, out_ref, inv_ref, all_ref):
    feats = own_ref.shape[0]
    places = slot_places(info_ref, tiles_ref.shape[0])
    side_by_side(all_ref, own_ref, pair_ref, other_ref)
    for b in range(tiles_ref.shape[0]):
        out = step_block(places, tiles_ref, own_ref, all_ref, b, True)
        inv = 1.0 / out[feats:feats + 8]
        inv_ref[b] = inv
        out_ref[:, b * TILE:(b + 1) * TILE] = (out[:feats] * inv[:1]).astype(jnp.bfloat16)


def second_kernel(info_ref, tiles_ref, own_ref, other_ref, pair_ref, inv_ref, extra_ref, out_ref, all_ref):
    places = slot_places(info_ref, tiles_ref.shape[0])
    side_by_side(all_ref, own_ref, pair_ref, other_ref)
    for b in range(tiles_ref.shape[0]):
        out = step_block(places, tiles_ref, own_ref, all_ref, b, False)
        out_ref[:, b * TILE:(b + 1) * TILE] = (out * inv_ref[b][:1]).astype(jnp.bfloat16)


def arch_kernel(info_ref, table_ref, r0, r1, r2, r3, v_ref, out_ref):
    blocks = v_ref.shape[1] // TILE
    narch = r0.shape[0]
    info = info_ref[...]
    me = info[META, 2]
    block = lax.div(column(table_ref[ARCH:ARCH + 1, :narch], narch), TILE) - info[META, 0]
    offsets = r0[:, 2 * TILE:].astype(jnp.float32)
    lane = lax.broadcasted_iota(jnp.int32, offsets.shape, 1)
    rows, places = [], []
    for p, r in enumerate((r0, r1, r2, r3)):
        for i in range(2):
            rows.append(r[:, i * TILE:(i + 1) * TILE].astype(jnp.float32))
            here = jnp.where(lane == 2 * (me ^ p) + i, offsets, 0.0)
            places.append(jnp.sum(here, axis=1, keepdims=True).astype(jnp.int32) + block)
    degree = jnp.sum(sum(rows), axis=1, keepdims=True)
    inv = jnp.where(degree > 0.0, 1.0 / degree, 0.0)
    rows = [r * inv for r in rows]
    weights = []
    for b in range(blocks):
        w = jnp.zeros((narch, TILE), jnp.float32)
        for r, place in zip(rows, places):
            w = w + jnp.where(place == b, r, 0.0)
        weights.append(jnp.concatenate(halves(w), axis=0))
    both = dot_last(jnp.concatenate(weights, axis=1), v_ref[...])
    part = both[:narch] + both[narch:]
    half = narch // 2
    out_ref[...] = jnp.concatenate([part[:half], part[half:]], axis=1)


def splat(x, shape):
    return jnp.broadcast_to(x, shape)


def solve_kernel(info_ref, total_ref, d0, d1, d2, d3, out_ref, copy_ref, whole_ref, scale_ref, made_ref, sem):
    total = total_ref[...].astype(jnp.bfloat16)
    feats, width = d0.shape
    n = total.shape[0] // 2
    same = pltpu.make_async_copy(d0, copy_ref, sem.at[0])
    same.start()
    me = info_ref[...][META, 2]
    step = 256
    for c in range(0, width, step):
        d = jnp.concatenate(in_order(me, [d[:, c:c + step] for d in (d0, d1, d2, d3)]), axis=0)
        whole_ref[:, c:c + step] = d
        wide = d.astype(jnp.float32)
        scale_ref[:, c:c + step] = lax.rsqrt(jnp.sum(wide * wide, axis=0, keepdims=True) / F + EPS)
    part = n // 2
    pieces = [total[p * part:(p + 1) * part] for p in range(4)]
    pieces = [jnp.concatenate([p[:, :feats], p[:, feats:]], axis=0) for p in pieces]
    pieces = in_order(me, pieces)
    arch = jnp.concatenate(pieces, axis=1)
    shape = (n, TILE)
    row = lax.broadcasted_iota(jnp.int32, shape, 0)
    col = lax.broadcasted_iota(jnp.int32, shape, 1)
    aug = jnp.concatenate([dot_last(arch, arch), jnp.zeros((n, TILE - n), jnp.float32)], axis=1)
    aug = aug + jnp.where(row + n == col, 1.0, 0.0)
    diagonal = jnp.zeros(shape, jnp.float32)
    group = 16
    for start in range(0, n, group):
        columns = [splat(aug[:, start + m:start + m + 1], shape) for m in range(group)]
        for m in range(group):
            k = start + m
            pivot = splat(columns[m][k:k + 1], shape)
            diagonal = jnp.where(row == k, pivot, diagonal)
            factor = jnp.where(row > k, columns[m] * (1.0 / pivot), 0.0)
            for later in range(m + 1, group):
                columns[later] = columns[later] - factor * splat(columns[later][k:k + 1], shape)
            aug = aug - factor * splat(aug[k:k + 1], shape)
    inverse = aug[:, n:2 * n] / jnp.sqrt(diagonal[:, :n])
    high, low = halves(inverse)
    third = (inverse - high.astype(jnp.float32) - low.astype(jnp.float32)).astype(jnp.bfloat16)
    q = dot(jnp.concatenate([high, low, third], axis=0), arch)
    q = jnp.concatenate(halves(q[:n] + q[n:2 * n] + q[2 * n:]), axis=0)
    copies = [same]
    for i, c in enumerate(range(0, width, step)):
        z = dot(q, whole_ref[:, c:c + step])
        made_ref[:, c:c + step] = (z[:n] + z[n:]) * scale_ref[:, c:c + step]
        copies.append(pltpu.make_async_copy(made_ref.at[:, c:c + step], out_ref.at[:, c:c + step], sem.at[1 + i]))
        copies[-1].start()
    for copy in copies:
        copy.wait()


def in_order(me, pieces):
    for bit in (1, 2):
        flip = (me & bit) == bit
        pieces = [jnp.where(flip, pieces[i ^ bit], pieces[i]) for i in range(4)]
    return pieces


def call(kernel, out_shape, kinds, args, flops, nbytes, scratch=(), limit=16, place=VMEM):
    single = not isinstance(out_shape, (list, tuple))
    spec = {"v": VMEM, "a": ANY, "h": HBM}
    return pl.pallas_call(
        kernel,
        out_shape=out_shape,
        in_specs=[spec[k] for k in kinds],
        out_specs=place if single else [place] * len(out_shape),
        scratch_shapes=scratch,
        compiler_params=pltpu.CompilerParams(vmem_limit_bytes=limit << 20),
        cost_estimate=pl.CostEstimate(flops=flops, bytes_accessed=nbytes, transcendentals=0),
    )(*args)


def exchange(matrix):
    size = lax.axis_size("cells")
    pairs = [(i, i ^ 1) for i in range(size)]
    others = [(i, i + 1) for i in range(1, size - 1, 2)]
    others = others + [(j, i) for i, j in others]
    return lax.ppermute(matrix, "cells", pairs), lax.ppermute(matrix, "cells", others)


def flip_feat(x, bits):
    return lax.ppermute(x, "feat", [(i, i ^ bits) for i in range(lax.axis_size("feat"))])


def on_device(expression, tiles, tile_cols, tile_counts, archetypes):
    blocks = tiles.shape[0]
    feats, rows = expression.shape
    narch = archetypes.shape[0]
    size = lax.axis_size("cells")
    cell, feat = lax.axis_index("cells"), lax.axis_index("feat")
    shape = jax.ShapeDtypeStruct
    bf16, f32 = jnp.bfloat16, jnp.float32
    line = lambda x: jnp.pad(x, ((0, 0), (0, TILE - x.shape[1])))
    numbers = jnp.stack([cell * blocks, cell & 1, feat]).astype(jnp.int32)
    info = jnp.concatenate([line(x) for x in (tile_cols.T, archetypes[None], tile_counts[None], numbers[None])], axis=0)
    flops = 2 * feats * TILE * TILE * NBT * blocks
    nbytes = 2 * TILE * TILE * NBT * blocks

    pair, other = exchange(expression)
    arch_rows, own = call(rows_kernel, [shape((narch, 3 * TILE), bf16), shape((feats, rows), bf16)], "vvhh",
                     (info, info, tiles, expression), 0, 0,
                     [pltpu.VMEM((blocks, 2, TILE, TILE), bf16), pltpu.SemaphoreType.DMA((3,))], 52)
    every = [pltpu.VMEM((feats, 3 * rows + TILE), bf16)]
    first, inv = call(first_kernel, [shape((feats, rows), bf16), shape((blocks, 8, TILE), f32)], "vvvvv",
                      (info, tiles, own, other, pair), flops, nbytes, every)

    row_pair, row_other = exchange(arch_rows)
    own_rows, _ = lax.optimization_barrier((arch_rows, other))
    near_rows, _ = lax.optimization_barrier((own_rows + row_pair + row_other, first))
    r = [near_rows] + [flip_feat(near_rows[:, :2 * TILE], p) for p in (1, 2, 3)]
    pair, other = exchange(first)
    part = call(arch_kernel, shape((narch // 2, 2 * feats), f32), "vvvvvvv", (info, info, *r, first), 0, 0)
    step = (info, tiles, first, other, pair, inv)
    diffused = call(second_kernel, shape((feats, rows), bf16), "vvvvvva", (*step, part), flops * 16, 0, every)
    seen, diffused = lax.optimization_barrier(([flip_feat(part, p) for p in (1, 2, 3)], diffused))
    part = jnp.concatenate([part, *seen], axis=0)
    flip_cells = lambda x, bits: lax.ppermute(x, "cells", [(i, i ^ bits) for i in range(size)])
    levels = (size - 1).bit_length()
    level = levels % 2
    if level:
        part = part + flip_cells(part, 1)

    pieces = [diffused, flip_feat(diffused, 1), flip_feat(diffused, 2)]
    pieces.append(flip_feat(pieces[2], 1))
    part, pieces[1] = lax.optimization_barrier((part, pieces[1]))
    while level < levels:
        near, far, both = (flip_cells(part, b << level) for b in (1, 2, 3))
        part = (part + near) + (far + both)
        level += 2
    coords, diffused = call(
        solve_kernel, [shape((narch, rows), f32), shape((feats, rows), bf16)], "vvvvvv",
        (info, part, *pieces), 4 * narch * F * rows, 4 * narch * rows,
        [pltpu.VMEM((4 * feats, rows), bf16), pltpu.VMEM((1, rows), f32), pltpu.VMEM((narch, rows), f32),
         pltpu.SemaphoreType.DMA((1 + rows // 256,))], place=HBM)
    return diffused, coords


def solution(mesh):
    return jax.shard_map(
        on_device,
        mesh=mesh,
        in_specs=(
            P("feat", "cells"),
            P("cells", None, None, None),
            P("cells", None),
            P("cells"),
            P(),
        ),
        out_specs=(P("feat", "cells"), P(None, "cells")),
        check_vma=False,
    )
```

```python
import functools
import jax
import jax.numpy as jnp
from jax import lax
from jax.experimental import pallas as pl
from jax.experimental.pallas import tpu as pltpu
from jax.sharding import PartitionSpec as P

F = 256
TILE = 128
NBT = 8
EPS = 1e-05
ARCH, COUNTS, META = range(NBT, NBT + 3)

VMEM = pl.BlockSpec(memory_space=pltpu.VMEM)
ANY = pl.BlockSpec(memory_space=pl.ANY)
HBM = pl.BlockSpec(memory_space=pltpu.HBM)


def dot_last(a, b):
    return lax.dot_general(a, b, (((1,), (1,)), ((), ())), preferred_element_type=jnp.float32)


def dot(a, b):
    return lax.dot_general(a, b, (((1,), (0,)), ((), ())), preferred_element_type=jnp.float32)


def lanes(block):
    return pl.ds(pl.multiple_of(block * TILE, TILE), TILE)


def wide_tile(tiles_ref, b, slots):
    return jnp.concatenate([tiles_ref[b, j] for j in slots], axis=1)


def halves(x):
    high = x.astype(jnp.bfloat16)
    return high, (x - high.astype(jnp.float32)).astype(jnp.bfloat16)


def column(row, narch):
    at = lax.broadcasted_iota(jnp.int32, (narch, narch), 0) == lax.broadcasted_iota(jnp.int32, (narch, narch), 1)
    return jnp.sum(jnp.where(at, row.astype(jnp.float32), 0.0), axis=1, keepdims=True).astype(jnp.int32)


def rows_kernel(info_ref, table_ref, tiles_ref, v_ref, rows_ref, own_ref, held_ref, sem):
    blocks = tiles_ref.shape[0]
    narch = rows_ref.shape[0]
    info = info_ref[...]
    first_block, first_slot = info[META, 0], 2 * info[META, 2]
    whole = pltpu.make_async_copy(v_ref, own_ref, sem.at[2])
    whole.start()
    copies = []
    for i in range(2):
        copies.append(pltpu.make_async_copy(tiles_ref.at[:, first_slot + i], held_ref.at[:, i], sem.at[i]))
        copies[-1].start()
    local = column(table_ref[ARCH:ARCH + 1, :narch], narch) - first_block * TILE
    at = lax.broadcasted_iota(jnp.int32, (narch, TILE), 1)
    hits = [(local - b * TILE) == at for b in range(blocks)]
    owner = lax.broadcasted_iota(jnp.int32, (narch, blocks), 1) == lax.div(local, TILE)
    owner = jnp.where(jnp.logical_and(owner, local >= 0), 1.0, 0.0).astype(jnp.bfloat16)
    cols = table_ref[:NBT, :blocks]
    steps = cols - first_block - lax.broadcasted_iota(jnp.int32, cols.shape, 1)
    steps = dot_last(owner, steps.astype(jnp.float32).astype(jnp.bfloat16))
    rows_ref[:, 2 * TILE:] = jnp.zeros((narch, TILE), jnp.bfloat16)
    rows_ref[:, 2 * TILE:2 * TILE + NBT] = steps.astype(jnp.bfloat16)
    for i in range(2):
        sel = [
            jnp.where(hit, jnp.where(first_slot + i < info[COUNTS, b], 1.0, 0.0), 0.0).astype(jnp.bfloat16)
            for b, hit in enumerate(hits)
        ]
        copies[i].wait()
        tall = jnp.concatenate([held_ref[b, i] for b in range(blocks)], axis=0)
        row = dot(jnp.concatenate(sel, axis=1), tall)
        rows_ref[:, i * TILE:(i + 1) * TILE] = row.astype(jnp.bfloat16)
    whole.wait()


def slot_places(info_ref, blocks):
    shape = (NBT, TILE)
    local = info_ref[:NBT] - info_ref[META:META + 1, :1]
    odd = jnp.broadcast_to(info_ref[META:META + 1, 1:2], shape)
    counts = jnp.broadcast_to(info_ref[COUNTS:COUNTS + 1], shape)
    below = jnp.where(odd == 1, 1, 2)
    lower, upper = local + (below + 1) * blocks, local - blocks + (3 - below) * blocks
    at = jnp.where(local < 0, lower, jnp.where(local >= blocks, upper, local))
    used = lax.broadcasted_iota(jnp.int32, shape, 0) < counts
    return jnp.where(used, at, 3 * blocks)


def side_by_side(all_ref, own_ref, pair_ref, other_ref):
    width = own_ref.shape[1]
    for i, ref in enumerate((own_ref, pair_ref, other_ref)):
        all_ref[:, i * width:(i + 1) * width] = ref[...]
    all_ref[:, 3 * width:] = jnp.zeros_like(all_ref[:, 3 * width:])


def step_block(places, tiles_ref, own_ref, all_ref, b, with_degree):
    blocks = tiles_ref.shape[0]
    parts, ones = [], []
    for j in range(NBT):
        at = places[j, b]
        parts.append(all_ref[:, lanes(at)] if j else own_ref[:, b * TILE:(b + 1) * TILE])
        if with_degree:
            used = jnp.where(at < 3 * blocks, 1.0, 0.0)
            ones.append(jnp.full((16, TILE), used, jnp.float32).astype(jnp.bfloat16))
    lhs = jnp.concatenate(parts, axis=1)
    if with_degree:
        lhs = jnp.concatenate([lhs, jnp.concatenate(ones, axis=1)], axis=0)
    return dot_last(lhs, wide_tile(tiles_ref, b, range(NBT)))


def first_kernel(info_ref, tiles_ref, own_ref, other_ref, pair_ref, out_ref, inv_ref, all_ref):
    feats = own_ref.shape[0]
    places = slot_places(info_ref, tiles_ref.shape[0])
    side_by_side(all_ref, own_ref, pair_ref, other_ref)
    for b in range(tiles_ref.shape[0]):
        out = step_block(places, tiles_ref, own_ref, all_ref, b, True)
        inv = 1.0 / out[feats:feats + 8]
        inv_ref[b] = inv
        out_ref[:, b * TILE:(b + 1) * TILE] = (out[:feats] * inv[:1]).astype(jnp.bfloat16)


def second_kernel(info_ref, tiles_ref, own_ref, other_ref, pair_ref, inv_ref, extra_ref, out_ref, all_ref):
    places = slot_places(info_ref, tiles_ref.shape[0])
    side_by_side(all_ref, own_ref, pair_ref, other_ref)
    for b in range(tiles_ref.shape[0]):
        out = step_block(places, tiles_ref, own_ref, all_ref, b, False)
        out_ref[:, b * TILE:(b + 1) * TILE] = (out * inv_ref[b][:1]).astype(jnp.bfloat16)


def arch_kernel(info_ref, table_ref, r0, r1, r2, r3, v_ref, out_ref):
    blocks = v_ref.shape[1] // TILE
    narch = r0.shape[0]
    info = info_ref[...]
    me = info[META, 2]
    block = lax.div(column(table_ref[ARCH:ARCH + 1, :narch], narch), TILE) - info[META, 0]
    offsets = r0[:, 2 * TILE:].astype(jnp.float32)
    lane = lax.broadcasted_iota(jnp.int32, offsets.shape, 1)
    rows, places = [], []
    for p, r in enumerate((r0, r1, r2, r3)):
        for i in range(2):
            rows.append(r[:, i * TILE:(i + 1) * TILE].astype(jnp.float32))
            here = jnp.where(lane == 2 * (me ^ p) + i, offsets, 0.0)
            places.append(jnp.sum(here, axis=1, keepdims=True).astype(jnp.int32) + block)
    degree = jnp.sum(sum(rows), axis=1, keepdims=True)
    inv = jnp.where(degree > 0.0, 1.0 / degree, 0.0)
    rows = [r * inv for r in rows]
    weights = []
    for b in range(blocks):
        w = jnp.zeros((narch, TILE), jnp.float32)
        for r, place in zip(rows, places):
            w = w + jnp.where(place == b, r, 0.0)
        weights.append(jnp.concatenate(halves(w), axis=0))
    both = dot_last(jnp.concatenate(weights, axis=1), v_ref[...])
    part = both[:narch] + both[narch:]
    half = narch // 2
    out_ref[...] = jnp.concatenate([part[:half], part[half:]], axis=1)


def splat(x, shape):
    return jnp.broadcast_to(x, shape)


def solve_kernel(info_ref, total_ref, d0, d1, d2, d3, out_ref, copy_ref, whole_ref, scale_ref, made_ref, sem):
    total = total_ref[...].astype(jnp.bfloat16)
    feats, width = d0.shape
    n = total.shape[0] // 2
    same = pltpu.make_async_copy(d0, copy_ref, sem.at[0])
    same.start()
    me = info_ref[...][META, 2]
    step = 512
    for c in range(0, width, step):
        d = jnp.concatenate(in_order(me, [d[:, c:c + step] for d in (d0, d1, d2, d3)]), axis=0)
        whole_ref[:, c:c + step] = d
        wide = d.astype(jnp.float32)
        scale_ref[:, c:c + step] = lax.rsqrt(jnp.sum(wide * wide, axis=0, keepdims=True) / F + EPS)
    part = n // 2
    pieces = [total[p * part:(p + 1) * part] for p in range(4)]
    pieces = [jnp.concatenate([p[:, :feats], p[:, feats:]], axis=0) for p in pieces]
    pieces = in_order(me, pieces)
    arch = jnp.concatenate(pieces, axis=1)
    shape = (n, TILE)
    row = lax.broadcasted_iota(jnp.int32, shape, 0)
    col = lax.broadcasted_iota(jnp.int32, shape, 1)
    aug = jnp.concatenate([dot_last(arch, arch), jnp.zeros((n, TILE - n), jnp.float32)], axis=1)
    aug = aug + jnp.where(row + n == col, 1.0, 0.0)
    diagonal = jnp.zeros(shape, jnp.float32)
    group = 16
    for start in range(0, n, group):
        columns = [splat(aug[:, start + m:start + m + 1], shape) for m in range(group)]
        for m in range(group):
            k = start + m
            pivot = splat(columns[m][k:k + 1], shape)
            diagonal = jnp.where(row == k, pivot, diagonal)
            factor = jnp.where(row > k, columns[m] * (1.0 / pivot), 0.0)
            for later in range(m + 1, group):
                columns[later] = columns[later] - factor * splat(columns[later][k:k + 1], shape)
            aug = aug - factor * splat(aug[k:k + 1], shape)
    inverse = aug[:, n:2 * n] / jnp.sqrt(diagonal[:, :n])
    high, low = halves(inverse)
    third = (inverse - high.astype(jnp.float32) - low.astype(jnp.float32)).astype(jnp.bfloat16)
    q = dot(jnp.concatenate([high, low, third], axis=0), arch)
    q = jnp.concatenate(halves(q[:n] + q[n:2 * n] + q[2 * n:]), axis=0)
    copies = [same]
    for i, c in enumerate(range(0, width, step)):
        z = dot(q, whole_ref[:, c:c + step])
        made_ref[:, c:c + step] = (z[:n] + z[n:]) * scale_ref[:, c:c + step]
        copies.append(pltpu.make_async_copy(made_ref.at[:, c:c + step], out_ref.at[:, c:c + step], sem.at[1 + i]))
        copies[-1].start()
    for copy in copies:
        copy.wait()


def in_order(me, pieces):
    for bit in (1, 2):
        flip = (me & bit) == bit
        pieces = [jnp.where(flip, pieces[i ^ bit], pieces[i]) for i in range(4)]
    return pieces


def call(kernel, out_shape, kinds, args, flops, nbytes, scratch=(), limit=16, place=VMEM):
    single = not isinstance(out_shape, (list, tuple))
    spec = {"v": VMEM, "a": ANY, "h": HBM}
    return pl.pallas_call(
        kernel,
        out_shape=out_shape,
        in_specs=[spec[k] for k in kinds],
        out_specs=place if single else [place] * len(out_shape),
        scratch_shapes=scratch,
        compiler_params=pltpu.CompilerParams(vmem_limit_bytes=limit << 20),
        cost_estimate=pl.CostEstimate(flops=flops, bytes_accessed=nbytes, transcendentals=0),
    )(*args)


def exchange(matrix):
    size = lax.axis_size("cells")
    pairs = [(i, i ^ 1) for i in range(size)]
    others = [(i, i + 1) for i in range(1, size - 1, 2)]
    others = others + [(j, i) for i, j in others]
    return lax.ppermute(matrix, "cells", pairs), lax.ppermute(matrix, "cells", others)


def flip_feat(x, bits):
    return lax.ppermute(x, "feat", [(i, i ^ bits) for i in range(lax.axis_size("feat"))])


def on_device(expression, tiles, tile_cols, tile_counts, archetypes):
    blocks = tiles.shape[0]
    feats, rows = expression.shape
    narch = archetypes.shape[0]
    size = lax.axis_size("cells")
    cell, feat = lax.axis_index("cells"), lax.axis_index("feat")
    shape = jax.ShapeDtypeStruct
    bf16, f32 = jnp.bfloat16, jnp.float32
    line = lambda x: jnp.pad(x, ((0, 0), (0, TILE - x.shape[1])))
    numbers = jnp.stack([cell * blocks, cell & 1, feat]).astype(jnp.int32)
    info = jnp.concatenate([line(x) for x in (tile_cols.T, archetypes[None], tile_counts[None], numbers[None])], axis=0)
    flops = 2 * feats * TILE * TILE * NBT * blocks
    nbytes = 2 * TILE * TILE * NBT * blocks

    pair, other = exchange(expression)
    arch_rows, own = call(rows_kernel, [shape((narch, 3 * TILE), bf16), shape((feats, rows), bf16)], "vvhh",
                     (info, info, tiles, expression), 0, 0,
                     [pltpu.VMEM((blocks, 2, TILE, TILE), bf16), pltpu.SemaphoreType.DMA((3,))], 52)
    every = [pltpu.VMEM((feats, 3 * rows + TILE), bf16)]
    first, inv = call(first_kernel, [shape((feats, rows), bf16), shape((blocks, 8, TILE), f32)], "vvvvv",
                      (info, tiles, own, other, pair), flops, nbytes, every)

    row_pair, row_other = exchange(arch_rows)
    own_rows, _ = lax.optimization_barrier((arch_rows, other))
    near_rows, _ = lax.optimization_barrier((own_rows + row_pair + row_other, first))
    r = [near_rows] + [flip_feat(near_rows[:, :2 * TILE], p) for p in (1, 2, 3)]
    pair, other = exchange(first)
    part = call(arch_kernel, shape((narch // 2, 2 * feats), f32), "vvvvvvv", (info, info, *r, first), 0, 0)
    step = (info, tiles, first, other, pair, inv)
    diffused = call(second_kernel, shape((feats, rows), bf16), "vvvvvva", (*step, part), flops * 16, 0, every)
    seen, diffused = lax.optimization_barrier(([flip_feat(part, p) for p in (1, 2, 3)], diffused))
    part = jnp.concatenate([part, *seen], axis=0)
    flip_cells = lambda x, bits: lax.ppermute(x, "cells", [(i, i ^ bits) for i in range(size)])
    levels = (size - 1).bit_length()
    level = levels % 2
    if level:
        part = part + flip_cells(part, 1)

    pieces = [diffused, flip_feat(diffused, 1), flip_feat(diffused, 2)]
    pieces.append(flip_feat(pieces[2], 1))
    part, pieces[1] = lax.optimization_barrier((part, pieces[1]))
    while level < levels:
        near, far, both = (flip_cells(part, b << level) for b in (1, 2, 3))
        part = (part + near) + (far + both)
        level += 2
    coords, diffused = call(
        solve_kernel, [shape((narch, rows), f32), shape((feats, rows), bf16)], "vvvvvv",
        (info, part, *pieces), 4 * narch * F * rows, 4 * narch * rows,
        [pltpu.VMEM((4 * feats, rows), bf16), pltpu.VMEM((1, rows), f32), pltpu.VMEM((narch, rows), f32),
         pltpu.SemaphoreType.DMA((1 + rows // 256,))], place=HBM)
    return diffused, coords


def solution(mesh):
    return jax.shard_map(
        on_device,
        mesh=mesh,
        in_specs=(
            P("feat", "cells"),
            P("cells", None, None, None),
            P("cells", None),
            P("cells"),
            P(),
        ),
        out_specs=(P("feat", "cells"), P(None, "cells")),
        check_vma=False,
    )
```
